256 devices in a mesh: gx: 16 (over x, y), gy: 8 (over z), gz: 2 (over core).
Axes of the slice: x: 4, y: 4, z: 8, core: 2. Of those that a mesh axis runs over, the one named last changes fastest.
Arguments:
- well_sources: float32 [12288, 64], P(('gx', 'gy'), 'gz'), may hold values from -6 to 6
- well_owner: int32 [12288, 1], P(('gx', 'gy')), may hold values from 0 to 127; in each aligned block of 96 rows (0 to 95, 96 to 191, ...) at most 2 rows name the same one
- well_cell: int32 [12288], P(('gx', 'gy')), may hold values from 0 to 2047
- flow_sign: int32 [3, 64, 256, 1024], P(None, 'gz', 'gx', 'gy'), may hold values from 0 to 7
- courant: float32 [3, 64, 256, 1024], P(None, 'gz', 'gx', 'gy'), may hold values from 0.01 to 0.3
- tracer: float32 [3, 64, 256, 1024], P(None, 'gz', 'gx', 'gy'), may hold values from -6 to 6
Outputs:
- lambda_start: float32 [64, 256, 1024], P('gz', 'gx', 'gy')
- smoothed: float32 [1024, 64, 256], P(('gx', 'gy', 'gz'))
The draws below stay inside these ranges and needn't reach their ends.
Inputs may be any that keep to these rules, and one draw needn't show every extreme that they name: `well_owner`: among the wells of one index of gx+gy at most 2 name the same owner, a bound that some block of them reaches.
All inputs are finite; a program needn't handle non-finite values.
Results may differ from the reference program's by a relative error of at most 0.00015.
Values sent between devices are 32-bit elements; how exact they have to be, the bound alone decides.
No kernel may reach another device: no remote copies, remote signals or barrier semaphores. Data moves between devices by JAX's collectives and lax.ppermute only.
A program may use at most 128 MiB of HBM per device.

```python
import math
import jax
import jax.numpy as jnp
import numpy as np
from jax import lax

CX = 16
CY = 128
STEPS = 3
WELL_DEV = 96
CAP = 2
NX = 256
NY = 1024
NZ = 64
WELLS = 12288
LX = 32
LY = 256
LZ = 64
N_GX = 16
N_GY = 8


def set_ends(drawn, own_key, least, largest):
    shape = drawn.shape
    index_at = [jax.random.randint(jax.random.fold_in(own_key, axis), (), 0, shape[axis]) for axis in range(len(shape))]
    drawn = drawn.at[tuple(index_at)].set(least)
    longest = shape.index(max(shape))
    index_at[longest] = (index_at[longest] + 1) % shape[longest]
    return drawn.at[tuple(index_at)].set(largest)


def levels(rng, dims, pieces, least, high):
    factor_of, own = 1.0, jax.random.fold_in(rng, 6)
    for dim, blocks in pieces:
        heights = jnp.exp(jax.random.uniform(jax.random.fold_in(own, dim), (blocks,), jnp.float32, least / len(pieces), high / len(pieces)))
        factor_of = factor_of * jnp.repeat(heights, dims[dim] // blocks).reshape([-1 if axis == dim else 1 for axis in range(len(dims))])
    return factor_of


def deal_out(key, own, number, rows, amount, top, limit, lean):
    sequence = jax.random.permutation(key, amount)
    crowded, common = load_shares(amount, rows * top, limit, lean, True), load_shares(amount, rows * top, limit, lean, False)
    places = jnp.arange(amount)

    def named(lengths, offset_by):
        used = int((lengths > 0).sum())
        fixed = max(1, used // 4)
        moved = fixed + (places - fixed + offset_by * (used - fixed)) % max(1, amount - fixed)
        return jnp.zeros((amount,), jnp.int32).at[sequence[jnp.where(places < fixed, places, moved)]].set(jnp.asarray(lengths, jnp.int32))

    lengths = jnp.where(number % 4 == 0, named(crowded, number // 4), named(common, number - number // 4 - 1))
    mixed = jax.random.permutation(jax.random.fold_in(own, 3), amount)
    giver, receiver = mixed[0:amount // 2 * 2:2], mixed[1:amount // 2 * 2:2]
    margin = jnp.minimum(lengths[giver] - 1, limit - lengths[receiver]) // 2
    margin = jnp.where((giver == sequence[0]) | (receiver == sequence[0]) | (lengths[receiver] == 0), 0, jnp.maximum(margin, 0))
    moved = jax.random.randint(jax.random.fold_in(own, 4), (amount // 2,), 0, 1 << 20) % (margin + 1)
    lengths = lengths.at[giver].add(-moved).at[receiver].add(moved)
    items = jnp.searchsorted(jnp.cumsum(lengths), jnp.arange(rows * top), side="right").astype(jnp.int32)
    grid = items.reshape(top, rows).T
    grid = grid[jax.random.permutation(jax.random.fold_in(own, 1), rows)]
    offset_by = jax.random.randint(jax.random.fold_in(own, 2), (rows, 1), 0, top)
    return jnp.take_along_axis(grid, (jnp.arange(top)[None, :] + offset_by) % top, axis=1)


def load_shares(amount, total, most, lean, full):
    weights = [(1 << 20) // math.isqrt(rank ** lean) + 1 for rank in range(1, amount + 1)]
    largest = most if full else min(most, max(-(-total // amount), total * weights[0] // sum(weights)))
    least = 1 if total - largest >= amount - 1 else 0
    counts, surplus = [largest] + [least] * (amount - 1), total - largest - least * (amount - 1)
    while surplus > 0:
        movable = [i for i in range(1, amount) if counts[i] < largest] or [i for i in range(1, amount) if counts[i] < most]
        pool, left = sum([weights[i] for i in movable]), surplus
        for i in movable:
            extra = min(most - counts[i], max(1, left * weights[i] // pool), surplus)
            counts[i] = counts[i] + extra
            surplus = surplus - extra
    return np.array(counts)


def normal_values(stream_key, shape, width, bound, cuts=(), kind=jnp.bfloat16):
    level = levels(stream_key, shape, cuts, -0.22, 0.18) if cuts else 1.0
    result = jax.random.normal(stream_key, shape, jnp.float32) * width * level
    return jnp.minimum(jnp.maximum(result, -bound), bound).astype(kind)


def setup_inputs(seed: int = 0) -> dict:
    arg_keys = jax.random.split(jax.random.key(seed), 7)
    well_sources = normal_values(arg_keys[0], (WELLS, NZ), 1.0, 6.0, ((0, 128), (1, 2)), jnp.float32)
    well_owner_keys = jax.random.split(jax.random.fold_in(arg_keys[1], 1), WELLS // WELL_DEV)
    well_owner_turns = jax.random.permutation(jax.random.fold_in(arg_keys[1], 3), WELLS // WELL_DEV)
    well_owner = jax.vmap(lambda own, number: deal_out(jax.random.fold_in(arg_keys[1], 2), own, number, WELL_DEV, N_GX * N_GY, 1, CAP, 2))(well_owner_keys, well_owner_turns).reshape((WELLS, 1))
    well_cell = set_ends(jax.random.randint(arg_keys[2], (WELLS,), 0, CX * CY), jax.random.fold_in(arg_keys[2], 1), 0, (CX * CY) - 1).astype(jnp.int32)
    flow_sign = set_ends(jax.random.randint(arg_keys[3], (STEPS, NZ, NX, NY), 0, 8), jax.random.fold_in(arg_keys[3], 1), 0, 7).astype(jnp.int32)
    courant = jnp.clip(jnp.exp(math.log(0.3) - 3.4011974 * jax.random.uniform(arg_keys[4], (3, NZ, NX, NY), jnp.float32) ** levels(arg_keys[4], (3, NZ, NX, NY), ((1, 2), (2, 16), (3, 8)), -0.2, 0.2)), 0.01, 0.3)
    tracer = normal_values(arg_keys[5], (STEPS, NZ, NX, NY), 1.0, 6.0, ((1, 2), (2, 16), (3, 8)), jnp.float32)
    return {"well_sources": well_sources, "well_owner": well_owner, "well_cell": well_cell, "flow_sign": flow_sign, "courant": courant, "tracer": tracer}


def correlation(extent, length):
    places = jnp.arange(extent).astype(jnp.float32)
    spacing = jnp.abs(places[:, None] - places[None, :])
    return jnp.exp(-spacing / length) / math.sqrt(length)

def from_above(values, along_dim):
    extent = values.shape[along_dim]
    inside = lax.slice_in_dim(values, 1, extent, axis=along_dim)
    border = jnp.zeros_like(lax.slice_in_dim(values, 0, 1, axis=along_dim))
    return jnp.concatenate([inside, border], axis=along_dim)

def from_below(values, along_dim):
    extent = values.shape[along_dim]
    inside = lax.slice_in_dim(values, 0, extent - 1, axis=along_dim)
    border = jnp.zeros_like(lax.slice_in_dim(values, 0, 1, axis=along_dim))
    return jnp.concatenate([border, inside], axis=along_dim)

def reference(well_sources, well_owner, well_cell, flow_sign, courant, tracer):
    owners = well_owner[:, 0]
    well_x = owners // N_GY * CX + well_cell // CY
    well_y = owners % N_GY * CY + well_cell % CY
    adjoint = jnp.zeros((NZ, NX, NY), jnp.float32).at[:, well_x, well_y].add(jnp.transpose(well_sources))
    staying = 1.0 - (courant[0] + courant[1] + courant[2])
    gradient = jnp.zeros((NZ, NX, NY), jnp.float32)
    for step in reversed(range(STEPS)):
        packed = flow_sign[step]
        updated = staying * adjoint
        for component, along_dim in ((0, 1), (1, 2), (2, 0)):
            upward = (packed // 2 ** component % 2).astype(jnp.float32)
            rising = courant[component] * upward
            falling = courant[component] * (1.0 - upward)
            updated = updated + from_above(rising * adjoint, along_dim) + from_below(falling * adjoint, along_dim)
        adjoint = updated
        gradient = gradient + adjoint * tracer[step]
    highest = lax.Precision.HIGHEST
    smooth_y = jnp.einsum('zxj,ij->zxi', gradient, correlation(NY, LY), precision=highest)
    smooth_x = jnp.einsum('zjy,ij->ziy', smooth_y, correlation(NX, LX), precision=highest)
    smoothed = jnp.einsum('jxy,ij->yix', smooth_x, correlation(NZ, LZ), precision=highest)
    return (adjoint, smoothed)
```

```python
import functools
import math

import jax
import jax.numpy as jnp
from jax import lax
from jax.experimental import pallas as pl
from jax.experimental.pallas import tpu as pltpu
from jax.sharding import PartitionSpec as P

F32 = jnp.float32
BF16 = jnp.bfloat16
CAP = 2


def iota(shape, dim):
    return lax.broadcasted_iota(jnp.int32, shape, dim)


def thirds(value):
    high = value.astype(BF16)
    left = value - high.astype(F32)
    middle = left.astype(BF16)
    low = (left - middle.astype(F32)).astype(BF16)
    return high, middle, low


def halves(value):
    high = value.astype(BF16)
    return high, (value - high.astype(F32)).astype(BF16)


def dot(left, right, dims):
    return lax.dot_general(left, right, (dims, ((), ())), preferred_element_type=F32)


def dot3(left, right, dims):
    lh, ll = halves(left)
    rh, rl = halves(right)
    return dot(lh, rh, dims) + (dot(lh, rl, dims) + dot(ll, rh, dims))


def dispatch_kernel(place_ref, sources_ref, owner_ref, cell_ref, out_ref):
    wells, depth = sources_ref.shape
    chunks, lanes = out_ref.shape
    half = lanes // CAP
    owner = owner_ref[...]
    owner_row = owner.astype(F32)
    owner_col = jnp.transpose(jnp.broadcast_to(owner_row, (8, wells)))[:, :1]
    earlier = iota((wells, wells), 0) < iota((wells, wells), 1)
    same = (owner_col == owner_row) & earlier
    rank = jnp.sum(same.astype(F32), axis=0, keepdims=True)
    target = (2 * owner + place_ref[2]).astype(F32)
    row = iota((chunks, wells), 0).astype(F32)
    cell_col = jnp.transpose(jnp.broadcast_to(cell_ref[...].astype(F32), (8, wells)))[:, :1]
    total = jnp.zeros((chunks, lanes), F32)
    payload = jnp.concatenate(
        [sources_ref[...], jnp.broadcast_to(cell_col, (wells, half - depth))], axis=1
    )
    blank = jnp.zeros((wells, half), F32)
    for slot in range(CAP):
        chosen = jnp.where((row == target) & (rank == float(slot)), 1.0, 0.0).astype(BF16)
        parts = [blank] * CAP
        parts[slot] = payload
        for piece in thirds(jnp.concatenate(parts, axis=1)):
            total = total + dot(chosen, piece, ((1,), (0,)))
    out_ref[...] = total


def landing(received_ref, depth, rows, lanes):
    pairs = received_ref.shape[0] // 2
    half = received_ref.shape[1] // CAP
    across = rows // depth
    received = received_ref[pl.ds(0, pairs, stride=2), :] + received_ref[pl.ds(1, pairs, stride=2), :]
    landed = jnp.zeros((rows, lanes), F32)
    pieces = thirds(received)
    for slot in range(CAP):
        cell = received[:, slot * half + depth : slot * half + depth + 1].astype(jnp.int32)
        spread = jnp.where(
            iota((2 * half, rows), 0) == slot * half + iota((2 * half, rows), 1) // across, 1.0, 0.0
        ).astype(BF16)
        at_x = iota((pairs, rows), 1) % across == cell // lanes
        at_y = jnp.where(iota((pairs, lanes), 1) == cell % lanes, 1.0, 0.0).astype(BF16)
        for piece in reversed(pieces):
            wide = jnp.where(at_x, dot(piece, spread, ((1,), (0,))), 0.0).astype(BF16)
            landed = landed + dot(wide, at_y, ((0,), (0,)))
    return landed


def spread_step(place_ref, adjoint, courant_ref, sign_ref, depth, faces):
    rows, lanes = adjoint.shape
    across = rows // depth
    xe_ref, xo_ref, ye_ref, yo_ref, z_ref = faces
    gx, gy, gz = place_ref[0], place_ref[1], place_ref[2]
    sign = sign_ref[0]
    row_x = iota((rows, lanes), 0) % across
    lane = iota((rows, lanes), 1)
    flow = [courant_ref[axis] * adjoint for axis in range(3)]
    rising = [jnp.where((sign & (1 << axis)) != 0, flow[axis], 0.0) for axis in range(3)]
    falling = [flow[axis] - rising[axis] for axis in range(3)]
    up = jnp.where(row_x == across - 1, 0.0, pltpu.roll(rising[0], rows - 1, 0))
    down = jnp.where(row_x == 0, 0.0, pltpu.roll(falling[0], 1, 0))
    rise3 = rising[0].reshape(depth, across, lanes)
    fall3 = falling[0].reshape(depth, across, lanes)
    low, high = rise3[:, 0, :], fall3[:, across - 1, :]
    even = (gx % 2) == 0
    xe_ref[...] = jnp.where(even, high, low)
    xo_ref[...] = jnp.where(even, low, high)
    staying = 1.0 - (courant_ref[0] + courant_ref[1] + courant_ref[2])
    kept = staying * adjoint + up + down
    up = jnp.where(lane == lanes - 1, 0.0, pltpu.roll(rising[1], lanes - 1, 1))
    down = jnp.where(lane == 0, 0.0, pltpu.roll(falling[1], 1, 1))
    ends = jnp.transpose(jnp.where(lane == 0, rising[1], falling[1]))
    low, high = ends[0:1, :], ends[lanes - 1 : lanes, :]
    even = (gy % 2) == 0
    ye_ref[...] = jnp.where(even, high, low)
    yo_ref[...] = jnp.where(even, low, high)
    kept = kept + up + down
    blank = jnp.zeros((across, lanes), F32)
    z_ref[...] = jnp.where(gz == 0, falling[2][rows - across :, :], rising[2][:across, :])
    kept = (
        kept
        + jnp.concatenate([rising[2][across:, :], blank], axis=0)
        + jnp.concatenate([blank, falling[2][: rows - across, :]], axis=0)
    )
    return kept


def first_kernel(place_ref, received_ref, courant_ref, sign_ref, kept_ref, *faces):
    rows, lanes = kept_ref.shape
    depth = faces[0].shape[0]
    adjoint = landing(received_ref, depth, rows, lanes)
    kept_ref[...] = spread_step(place_ref, adjoint, courant_ref, sign_ref, depth, faces)


def join(place_ref, kept_ref, xe_ref, xo_ref, ye_ref, yo_ref, z_ref, sizes):
    rows, lanes = kept_ref.shape
    depth = xe_ref.shape[0]
    across = rows // depth
    gx, gy, gz = place_ref[0], place_ref[1], place_ref[2]
    even = (gx % 2) == 0
    xe, xo = xe_ref[...], xo_ref[...]
    above = jnp.where(gx == sizes[0] - 1, 0.0, jnp.where(even, xe, xo))
    below = jnp.where(gx == 0, 0.0, jnp.where(even, xo, xe))
    row_x = iota((depth, across, lanes), 1)
    adjoint = kept_ref[...] + jnp.where(
        row_x == across - 1,
        above[:, None, :],
        jnp.where(row_x == 0, below[:, None, :], 0.0),
    ).reshape(rows, lanes)
    even = (gy % 2) == 0
    ye, yo = ye_ref[...], yo_ref[...]
    above = jnp.where(gy == sizes[1] - 1, 0.0, jnp.where(even, ye, yo))
    below = jnp.where(gy == 0, 0.0, jnp.where(even, yo, ye))
    row_y = iota((lanes, rows), 0)
    adjoint = adjoint + jnp.transpose(
        jnp.where(row_y == lanes - 1, above, jnp.where(row_y == 0, below, 0.0))
    )
    z = z_ref[...]
    blank = jnp.zeros((rows - across, lanes), F32)
    adjoint = adjoint + jnp.where(
        gz == 0,
        jnp.concatenate([blank, z], axis=0),
        jnp.concatenate([z, blank], axis=0),
    )
    return adjoint


def middle_kernel(
    sizes, has_gradient, place_ref, kept_ref, xe, xo, ye, yo, z, courant_ref, sign_ref, tracer_ref, *rest
):
    gradient_in = None
    if has_gradient:
        gradient_in, *rest = rest
    kept_out, gradient_ref, *faces = rest
    adjoint = join(place_ref, kept_ref, xe, xo, ye, yo, z, sizes)
    kept_out[...] = spread_step(place_ref, adjoint, courant_ref, sign_ref, xe.shape[0], faces)
    gradient = adjoint * tracer_ref[0]
    gradient_ref[...] = gradient + gradient_in[...] if has_gradient else gradient


def last_kernel(
    sizes, place_ref, kept_ref, xe, xo, ye, yo, z, tracer_ref, gradient_in, adjoint_ref, lines_ref, work_ref
):
    rows = kept_ref.shape[0]
    depth = xe.shape[0]
    across = rows // depth
    adjoint = join(place_ref, kept_ref, xe, xo, ye, yo, z, sizes)
    adjoint_ref[...] = adjoint
    work_ref[...] = gradient_in[...] + adjoint * tracer_ref[0]
    for x in range(across):
        lines_ref[x * depth : (x + 1) * depth, :] = work_ref[pl.ds(x, depth, stride=across), :]


def smooth_y_kernel(depth, length, rows_each, lines_ref, out_ref):
    rows, lanes = lines_ref.shape
    lines = lines_ref[...]
    share = 2 * depth
    groups = lanes // rows_each
    scale = 1.0 / math.sqrt(length)
    order = iota((lanes, lanes), 0)
    y_out = (order % groups) * rows_each + order // groups
    table = jnp.exp(-jnp.abs(y_out - iota((lanes, lanes), 1)).astype(F32) / length) * scale
    side = iota((8, lanes), 0)
    y_in = iota((8, lanes), 1)
    carry_table = jnp.exp(-jnp.where(side == 0, lanes - 1 - y_in, y_in).astype(F32) / length) * scale
    both = dot3(jnp.concatenate([table, carry_table], axis=0), lines, ((1,), (1,)))
    result, carry = both[:lanes], both[lanes:]
    place = iota((8, rows), 1)
    decay = math.exp(-lanes / length)
    right = carry
    left = carry
    step = share
    factor = decay
    while step < rows:
        right = right + factor * jnp.where(place >= step, pltpu.roll(right, step, 1), 0.0)
        left = left + factor * jnp.where(place < rows - step, pltpu.roll(left, rows - step, 1), 0.0)
        step, factor = 2 * step, factor * factor
    right = jnp.where(place >= share, pltpu.roll(right, share, 1), 0.0)[0:1, :]
    left = jnp.where(place < rows - share, pltpu.roll(left, rows - share, 1), 0.0)[1:2, :]
    row = iota((lanes, 1), 0)
    y_row = ((row % groups) * rows_each + row // groups).astype(F32)
    result = (
        result + jnp.exp(-(y_row + 1.0) / length) * right + jnp.exp(-(lanes - y_row) / length) * left
    )
    per_tile = lanes // depth
    quarter = iota((groups, lanes), 1) // depth
    for tile in range(rows // lanes):
        pieces = [
            result[r * groups : (r + 1) * groups, tile * lanes : (tile + 1) * lanes]
            for r in range(rows_each)
        ]
        for u in range(per_tile):
            line = tile * per_tile + u
            block, xx = line // 2, line % 2
            chunk = jnp.zeros((groups, lanes), F32)
            for r in range(rows_each):
                turn = ((r - u) * depth) % lanes
                piece = pltpu.roll(pieces[r], turn, 1) if turn else pieces[r]
                chunk = jnp.where(quarter == r, piece, chunk)
            out_ref[pl.ds(block * 2 * groups + xx, groups, stride=2), :] = chunk


def smooth_xz_kernel(depth, length_x, length_z, rows_each, data_ref, out_ref):
    rows, lanes = data_ref.shape
    full_x = out_ref.shape[1]
    sources = rows // 4
    part = [jnp.zeros((lanes, full_x), F32) for _ in range(2)]
    for xx in range(2):
        x_in = 2 * iota((sources, full_x), 0) + xx
        table = jnp.exp(-jnp.abs(x_in - iota((sources, full_x), 1)).astype(F32) / length_x)
        table = table * (1.0 / math.sqrt(length_x))
        for g in range(2):
            block = data_ref[pl.ds(2 * g + xx, sources, stride=4), :]
            part[g] = part[g] + dot3(block, table, ((0,), (0,)))
    full_z = 2 * depth
    total = None
    for g in range(2):
        r_out, z_out = iota((rows_each * full_z, lanes), 0) // full_z, iota((rows_each * full_z, lanes), 0) % full_z
        r_in, z_in = iota((rows_each * full_z, lanes), 1) // depth, iota((rows_each * full_z, lanes), 1) % depth
        table = jnp.exp(-jnp.abs(z_out - z_in - g * depth).astype(F32) / length_z) * (1.0 / math.sqrt(length_z))
        table = jnp.where(r_out == r_in, table, 0.0)
        term = dot3(table, part[g], ((1,), (0,)))
        total = term if total is None else total + term
    out_ref[...] = total


def pair_swaps(count):
    even = [(i, i ^ 1) for i in range(count)]
    odd = [(i, (i + 1) % count) for i in range(1, count, 2)]
    odd = odd + [(target, source) for source, target in odd]
    return even, odd


def exchange(faces):
    xe, xo, ye, yo, z = faces
    x_even, x_odd = pair_swaps(lax.axis_size("gx"))
    y_even, y_odd = pair_swaps(lax.axis_size("gy"))
    return (
        lax.ppermute(xe, "gx", x_even),
        lax.ppermute(xo, "gx", x_odd),
        lax.ppermute(ye, "gy", y_even),
        lax.ppermute(yo, "gy", y_odd),
        lax.ppermute(z, "gz", [(0, 1), (1, 0)]),
    )


def per_device(well_sources, well_owner, well_cell, flow_sign, courant, tracer):
    steps, brick_z, brick_x, brick_y = flow_sign.shape
    wells = well_sources.shape[0]
    rows = brick_z * brick_x
    sizes = (lax.axis_size("gx"), lax.axis_size("gy"), lax.axis_size("gz"))
    devices = sizes[0] * sizes[1] * sizes[2]
    place = jnp.stack([lax.axis_index("gx"), lax.axis_index("gy"), lax.axis_index("gz")])
    axes = ("gx", "gy", "gz")
    smem = pl.BlockSpec(memory_space=pltpu.SMEM)
    vmem = pl.BlockSpec(memory_space=pltpu.VMEM)

    def shape(*dims):
        return jax.ShapeDtypeStruct(dims, F32)

    def step_spec(step):
        return pl.BlockSpec((1, rows, brick_y), lambda i, step=step: (step, 0, 0))

    def whole(*dims):
        return pl.BlockSpec(dims, lambda i: (0,) * len(dims))

    outgoing = pl.pallas_call(
        dispatch_kernel,
        in_specs=[smem, vmem, vmem, vmem],
        out_specs=vmem,
        out_shape=shape(devices, 128),
        name="dispatch",
    )(place, well_sources, well_owner.reshape(1, wells), well_cell.reshape(1, wells))
    received = lax.all_to_all(outgoing, axes, split_axis=0, concat_axis=0, tiled=True)

    flow = flow_sign.reshape(steps, rows, brick_y)
    speed = courant.reshape(3, rows, brick_y)
    trace = tracer.reshape(steps, rows, brick_y)
    face_shapes = [
        shape(brick_z, brick_y),
        shape(brick_z, brick_y),
        shape(1, rows),
        shape(1, rows),
        shape(brick_x, brick_y),
    ]
    face_specs = [whole(*f.shape) for f in face_shapes]
    field = whole(rows, brick_y)
    speed_spec = whole(3, rows, brick_y)
    kept, *faces = pl.pallas_call(
        first_kernel,
        grid=(1,),
        in_specs=[smem, whole(devices, 128), speed_spec, step_spec(steps - 1)],
        out_specs=[field] + face_specs,
        out_shape=[shape(rows, brick_y)] + face_shapes,
        name="first",
    )(place, received, speed, flow)
    gradient = []
    for step in reversed(range(1, steps)):
        arrived = exchange(faces)
        kept, grown, *faces = pl.pallas_call(
            functools.partial(middle_kernel, sizes, bool(gradient)),
            grid=(1,),
            in_specs=[smem, field] + face_specs + [speed_spec, step_spec(step - 1), step_spec(step)]
            + [field] * len(gradient),
            out_specs=[field, field] + face_specs,
            out_shape=[shape(rows, brick_y)] * 2 + face_shapes,
            name=f"step{step}",
        )(place, kept, *arrived, speed, flow, trace, *gradient)
        gradient = [grown]
    arrived = exchange(faces)
    adjoint, lines = pl.pallas_call(
        functools.partial(last_kernel, sizes),
        grid=(1,),
        in_specs=[smem, field] + face_specs + [step_spec(0), field],
        out_specs=[field, field],
        out_shape=[shape(rows, brick_y)] * 2,
        scratch_shapes=[pltpu.VMEM((rows, brick_y), F32)],
        name="step0",
    )(place, kept, *arrived, trace, *gradient)

    y_lines = lax.all_to_all(
        lines.reshape(sizes[1], rows // sizes[1], brick_y), "gy", split_axis=0, concat_axis=0, tiled=True
    ).reshape(rows, brick_y)
    rows_each = sizes[1] * brick_y // devices
    smooth = pl.pallas_call(
        functools.partial(smooth_y_kernel, brick_z, 2.0 * brick_y, rows_each),
        in_specs=[vmem],
        out_specs=vmem,
        out_shape=shape(rows, brick_y),
        name="smooth_y",
    )(y_lines)
    planes = lax.all_to_all(
        smooth.reshape(devices, 2, 128), axes, split_axis=0, concat_axis=0, tiled=True
    ).reshape(rows, brick_y)
    full_x, full_z = sizes[0] * brick_x, sizes[2] * brick_z
    smoothed = pl.pallas_call(
        functools.partial(smooth_xz_kernel, brick_z, 2.0 * brick_x, 2.0 * brick_z, rows_each),
        in_specs=[vmem],
        out_specs=vmem,
        out_shape=shape(rows_each * full_z, full_x),
        name="smooth_xz",
    )(planes)
    return (
        adjoint.reshape(brick_z, brick_x, brick_y),
        smoothed.reshape(rows_each, full_z, full_x),
    )


def solution(mesh):
    return jax.shard_map(
        per_device,
        mesh=mesh,
        in_specs=(
            P(("gx", "gy"), "gz"),
            P(("gx", "gy"), None),
            P(("gx", "gy")),
            P(None, "gz", "gx", "gy"),
            P(None, "gz", "gx", "gy"),
            P(None, "gz", "gx", "gy"),
        ),
        out_specs=(P("gz", "gx", "gy"), P(("gx", "gy", "gz"), None, None)),
        check_vma=False,
    )
```

```python
import functools
import math

import jax
import jax.numpy as jnp
from jax import lax
from jax.experimental import pallas as pl
from jax.experimental.pallas import tpu as pltpu
from jax.sharding import PartitionSpec as P

F32 = jnp.float32
BF16 = jnp.bfloat16
CAP = 2


def iota(shape, dim):
    return lax.broadcasted_iota(jnp.int32, shape, dim)


def thirds(value):
    high = value.astype(BF16)
    left = value - high.astype(F32)
    middle = left.astype(BF16)
    low = (left - middle.astype(F32)).astype(BF16)
    return high, middle, low


def halves(value):
    high = value.astype(BF16)
    return high, (value - high.astype(F32)).astype(BF16)


def dot(left, right, dims):
    return lax.dot_general(left, right, (dims, ((), ())), preferred_element_type=F32)


def dot3(left, right, dims):
    lh, ll = halves(left)
    rh, rl = halves(right)
    return dot(lh, rh, dims) + (dot(lh, rl, dims) + dot(ll, rh, dims))


def fetch(copies, sems):
    started = [pltpu.make_async_copy(source, target, sems.at[i]) for i, (source, target) in enumerate(copies)]
    for copy in started:
        copy.start()
    return started


def dispatch_kernel(sources_hbm, owner_hbm, cell_hbm, out_ref, sources_ref, owner_ref, cell_ref, sems):
    for copy in fetch([(sources_hbm, sources_ref), (owner_hbm, owner_ref), (cell_hbm, cell_ref)], sems):
        copy.wait()
    depth, wells = sources_ref.shape
    chunks, lanes = out_ref.shape
    owner = owner_ref[...]
    owner_row = owner.astype(F32)
    owner_col = jnp.transpose(jnp.broadcast_to(owner_row, (8, wells)))[:, :1]
    earlier = iota((wells, wells), 0) < iota((wells, wells), 1)
    same = (owner_col == owner_row) & earlier
    rank = jnp.sum(same.astype(F32), axis=0, keepdims=True)
    target = CAP * owner_row + rank
    chosen = jnp.where(iota((chunks, wells), 0).astype(F32) == target, 1.0, 0.0).astype(BF16)
    cell = jnp.broadcast_to(cell_ref[...].astype(F32), (lanes - depth, wells))
    total = jnp.zeros((chunks, lanes), F32)
    for piece in thirds(jnp.concatenate([sources_ref[...], cell], axis=0)):
        total = total + dot(chosen, piece, ((1,), (1,)))
    out_ref[...] = total


def landing(received_ref, depth, rows, lanes):
    wells, width = received_ref.shape
    across = rows // depth
    received = received_ref[...]
    cell = received[:, depth : depth + 1].astype(jnp.int32)
    spread = jnp.where(iota((width, rows), 0) == iota((width, rows), 1) // across, 1.0, 0.0).astype(BF16)
    at_x = iota((wells, rows), 1) % across == cell // lanes
    at_y = jnp.where(iota((wells, lanes), 1) == cell % lanes, 1.0, 0.0).astype(BF16)
    landed = jnp.zeros((rows, lanes), F32)
    for piece in reversed(thirds(received)):
        wide = jnp.where(at_x, dot(piece, spread, ((1,), (0,))), 0.0).astype(BF16)
        landed = landed + dot(wide, at_y, ((0,), (0,)))
    return landed


def put_faces(adjoint, step, courant_ref, sign_ref, depth, faces):
    rows, lanes = adjoint.shape
    across = rows // depth
    xe_ref, xo_ref, ye_ref, yo_ref, z_ref = faces
    sign = sign_ref[step]
    lane = iota((rows, lanes), 1)
    flow = courant_ref[1] * adjoint
    raised = (sign & 2) != 0
    ends = jnp.transpose(jnp.where(raised == (lane == 0), flow, 0.0))
    low, high = ends[0:1, :], ends[lanes - 1 : lanes, :]
    even = (lax.axis_index("gy") % 2) == 0
    ye_ref[...] = jnp.where(even, high, low)
    yo_ref[...] = jnp.where(even, low, high)
    shape = (depth, across, lanes)
    flow = (courant_ref[0] * adjoint).reshape(shape)
    raised = (sign & 1).reshape(shape)
    low = jnp.where(raised[:, 0, :] != 0, flow[:, 0, :], 0.0)
    high = jnp.where(raised[:, across - 1, :] != 0, 0.0, flow[:, across - 1, :])
    even = (lax.axis_index("gx") % 2) == 0
    xe_ref[...] = jnp.where(even, high, low)
    xo_ref[...] = jnp.where(even, low, high)
    flow = courant_ref[2]
    low = jnp.where((sign[:across] & 4) != 0, flow[:across] * adjoint[:across], 0.0)
    high = jnp.where((sign[rows - across :] & 4) != 0, 0.0, flow[rows - across :] * adjoint[rows - across :])
    z_ref[...] = jnp.where(lax.axis_index("gz") == 0, high, low)


def inner_kernel(step, depth, tracer_step, adjoint_ref, courant_ref, sign_ref, *rest):
    gradient_in, tracer_ref, gradient_ref = None, None, None
    if tracer_step is not None:
        tracer_ref, *rest = rest
        if len(rest) == 3:
            gradient_in, *rest = rest
        gradient_ref, *rest = rest
    (kept_ref,) = rest
    adjoint = adjoint_ref[...]
    rows, lanes = adjoint.shape
    across = rows // depth
    sign = sign_ref[step]
    row_x = iota((rows, lanes), 0) % across
    lane = iota((rows, lanes), 1)
    flow = [courant_ref[axis] * adjoint for axis in range(3)]
    rising = [jnp.where((sign & (1 << axis)) != 0, flow[axis], 0.0) for axis in range(3)]
    falling = [flow[axis] - rising[axis] for axis in range(3)]
    kept = (1.0 - (courant_ref[0] + courant_ref[1] + courant_ref[2])) * adjoint
    up = jnp.where(row_x == across - 1, 0.0, pltpu.roll(rising[0], rows - 1, 0))
    down = jnp.where(row_x == 0, 0.0, pltpu.roll(falling[0], 1, 0))
    kept = kept + up + down
    up = jnp.where(lane == lanes - 1, 0.0, pltpu.roll(rising[1], lanes - 1, 1))
    down = jnp.where(lane == 0, 0.0, pltpu.roll(falling[1], 1, 1))
    kept = kept + up + down
    blank = jnp.zeros((across, lanes), F32)
    kept_ref[...] = (
        kept
        + jnp.concatenate([rising[2][across:, :], blank], axis=0)
        + jnp.concatenate([blank, falling[2][: rows - across, :]], axis=0)
    )
    if tracer_step is not None:
        gradient = adjoint * tracer_ref[tracer_step]
        gradient_ref[...] = gradient if gradient_in is None else gradient_in[...] + gradient


def first_kernel(step, received_ref, courant_hbm, sign_hbm, *rest):
    adjoint_ref, *faces, courant_ref, sign_ref, sems = rest
    rows, lanes = adjoint_ref.shape
    depth = faces[0].shape[0]
    across = rows // depth
    last = rows - across
    copies = fetch(
        [
            (courant_hbm.at[1], courant_ref.at[1]),
            (sign_hbm.at[step], sign_ref.at[0]),
            (courant_hbm.at[0], courant_ref.at[0]),
            (courant_hbm.at[2, 0:across], courant_ref.at[2, 0:across]),
            (courant_hbm.at[2, last:rows], courant_ref.at[2, last:rows]),
        ],
        sems,
    )
    adjoint = landing(received_ref, depth, rows, lanes)
    adjoint_ref[...] = adjoint
    for copy in copies:
        copy.wait()
    put_faces(adjoint, 0, courant_ref, sign_ref, depth, faces)


def join(sizes, kept_ref, xe_ref, xo_ref, ye_ref, yo_ref, z_ref):
    rows, lanes = kept_ref.shape
    depth = xe_ref.shape[0]
    across = rows // depth
    gx, gy, gz = lax.axis_index("gx"), lax.axis_index("gy"), lax.axis_index("gz")
    even = (gx % 2) == 0
    xe, xo = xe_ref[...], xo_ref[...]
    above = jnp.where(gx == sizes[0] - 1, 0.0, jnp.where(even, xe, xo))
    below = jnp.where(gx == 0, 0.0, jnp.where(even, xo, xe))
    row_x = iota((depth, across, lanes), 1)
    adjoint = kept_ref[...] + jnp.where(
        row_x == across - 1,
        above[:, None, :],
        jnp.where(row_x == 0, below[:, None, :], 0.0),
    ).reshape(rows, lanes)
    even = (gy % 2) == 0
    ye, yo = ye_ref[...], yo_ref[...]
    above = jnp.where(gy == sizes[1] - 1, 0.0, jnp.where(even, ye, yo))
    below = jnp.where(gy == 0, 0.0, jnp.where(even, yo, ye))
    row_y = iota((lanes, rows), 0)
    adjoint = adjoint + jnp.transpose(
        jnp.where(row_y == lanes - 1, above, jnp.where(row_y == 0, below, 0.0))
    )
    z = z_ref[...]
    blank = jnp.zeros((rows - across, lanes), F32)
    return adjoint + jnp.where(
        gz == 0,
        jnp.concatenate([blank, z], axis=0),
        jnp.concatenate([z, blank], axis=0),
    )


def middle_kernel(sizes, step, kept_ref, xe, xo, ye, yo, z, courant_ref, sign_ref, adjoint_ref, *faces):
    adjoint = join(sizes, kept_ref, xe, xo, ye, yo, z)
    adjoint_ref[...] = adjoint
    put_faces(adjoint, step, courant_ref, sign_ref, xe.shape[0], faces)


def last_kernel(
    sizes, kept_ref, xe, xo, ye, yo, z, tracer_ref, gradient_in, adjoint_ref, lines_ref, work_ref
):
    rows = kept_ref.shape[0]
    depth = xe.shape[0]
    across = rows // depth
    adjoint = join(sizes, kept_ref, xe, xo, ye, yo, z)
    adjoint_ref[...] = adjoint
    work_ref[...] = gradient_in[...] + adjoint * tracer_ref[0]
    for x in range(across):
        lines_ref[x * depth : (x + 1) * depth, :] = work_ref[pl.ds(x, depth, stride=across), :]


def smooth_y_kernel(depth, length, rows_each, lines_ref, out_ref):
    rows, lanes = lines_ref.shape
    lines = lines_ref[...]
    share = 2 * depth
    groups = lanes // rows_each
    scale = 1.0 / math.sqrt(length)
    order = iota((lanes, lanes), 0)
    y_out = (order % groups) * rows_each + order // groups
    table = jnp.exp(-jnp.abs(y_out - iota((lanes, lanes), 1)).astype(F32) / length) * scale
    side = iota((8, lanes), 0)
    y_in = iota((8, lanes), 1)
    carry_table = jnp.exp(-jnp.where(side == 0, lanes - 1 - y_in, y_in).astype(F32) / length) * scale
    both = dot3(jnp.concatenate([table, carry_table], axis=0), lines, ((1,), (1,)))
    result, carry = both[:lanes], both[lanes:]
    place = iota((8, rows), 1)
    decay = math.exp(-lanes / length)
    right = carry
    left = carry
    step = share
    factor = decay
    while step < rows:
        right = right + factor * jnp.where(place >= step, pltpu.roll(right, step, 1), 0.0)
        left = left + factor * jnp.where(place < rows - step, pltpu.roll(left, rows - step, 1), 0.0)
        step, factor = 2 * step, factor * factor
    right = jnp.where(place >= share, pltpu.roll(right, share, 1), 0.0)[0:1, :]
    left = jnp.where(place < rows - share, pltpu.roll(left, rows - share, 1), 0.0)[1:2, :]
    row = iota((lanes, 1), 0)
    y_row = ((row % groups) * rows_each + row // groups).astype(F32)
    result = (
        result + jnp.exp(-(y_row + 1.0) / length) * right + jnp.exp(-(lanes - y_row) / length) * left
    )
    per_tile = lanes // depth
    quarter = iota((groups, lanes), 1) // depth
    for tile in range(rows // lanes):
        pieces = [
            result[r * groups : (r + 1) * groups, tile * lanes : (tile + 1) * lanes]
            for r in range(rows_each)
        ]
        for u in range(per_tile):
            line = tile * per_tile + u
            block, xx = line // 2, line % 2
            chunk = jnp.zeros((groups, lanes), F32)
            for r in range(rows_each):
                turn = ((r - u) * depth) % lanes
                piece = pltpu.roll(pieces[r], turn, 1) if turn else pieces[r]
                chunk = jnp.where(quarter == r, piece, chunk)
            out_ref[pl.ds(block * 2 * groups + xx, groups, stride=2), :] = chunk


def smooth_xz_kernel(depth, length_x, length_z, rows_each, data_ref, out_hbm, work_ref, sems):
    rows, lanes = data_ref.shape
    full_x = work_ref.shape[1]
    sources = rows // 4
    part = [jnp.zeros((lanes, full_x), F32) for _ in range(2)]
    for xx in range(2):
        x_in = 2 * iota((sources, full_x), 0) + xx
        table = jnp.exp(-jnp.abs(x_in - iota((sources, full_x), 1)).astype(F32) / length_x)
        table = table * (1.0 / math.sqrt(length_x))
        for g in range(2):
            block = data_ref[pl.ds(2 * g + xx, sources, stride=4), :]
            part[g] = part[g] + dot3(block, table, ((0,), (0,)))
    full_z = 2 * depth
    z_out, z_in = iota((full_z, full_z), 0), iota((full_z, full_z), 1)
    table = jnp.exp(-jnp.abs(z_out - z_in).astype(F32) / length_z) * (1.0 / math.sqrt(length_z))
    copies = []
    for r in range(rows_each):
        column = jnp.concatenate([part[g][r * depth : (r + 1) * depth] for g in range(2)], axis=0)
        here = slice(r * full_z, (r + 1) * full_z)
        work_ref[here, :] = dot3(table, column, ((1,), (0,)))
        copy = pltpu.make_async_copy(work_ref.at[here], out_hbm.at[here], sems.at[r])
        copy.start()
        copies.append(copy)
    for copy in copies:
        copy.wait()


def pair_swaps(count):
    even = [(i, i ^ 1) for i in range(count)]
    odd = [(i, (i + 1) % count) for i in range(1, count, 2)]
    odd = odd + [(target, source) for source, target in odd]
    return even, odd


def exchange(faces):
    xe, xo, ye, yo, z = faces
    x_even, x_odd = pair_swaps(lax.axis_size("gx"))
    y_even, y_odd = pair_swaps(lax.axis_size("gy"))
    return (
        lax.ppermute(xe, "gx", x_even),
        lax.ppermute(xo, "gx", x_odd),
        lax.ppermute(ye, "gy", y_even),
        lax.ppermute(yo, "gy", y_odd),
        lax.ppermute(z, "gz", [(0, 1), (1, 0)]),
    )


def local(kernel, name, inputs, outputs, scratch=(), far=0, far_out=False):
    vmem = pl.BlockSpec(memory_space=pltpu.VMEM)
    hbm = pl.BlockSpec(memory_space=pl.ANY)
    near = len(inputs) - far
    return pl.pallas_call(
        kernel,
        in_specs=[vmem] * near + [hbm] * far,
        out_specs=[hbm if far_out else vmem] * len(outputs),
        out_shape=[(pltpu.HBM if far_out else pltpu.VMEM)(dims, F32) for dims in outputs],
        scratch_shapes=scratch,
        compiler_params=pltpu.CompilerParams(vmem_limit_bytes=8 << 20),
        name=name,
    )(
        *[pltpu.with_memory_space_constraint(values, pltpu.VMEM) for values in inputs[:near]],
        *[pltpu.with_memory_space_constraint(values, pltpu.HBM) for values in inputs[near:]],
    )


def per_device(well_sources, well_owner, well_cell, flow_sign, courant, tracer):
    steps, brick_z, brick_x, brick_y = flow_sign.shape
    wells = well_sources.shape[0]
    rows = brick_z * brick_x
    sizes = (lax.axis_size("gx"), lax.axis_size("gy"), lax.axis_size("gz"))
    devices = sizes[0] * sizes[1] * sizes[2]
    owners = sizes[0] * sizes[1]
    axes = ("gx", "gy", "gz")
    (outgoing,) = local(
        dispatch_kernel,
        "dispatch",
        [well_sources.T, well_owner.reshape(1, wells), well_cell.reshape(1, wells)],
        [(CAP * owners, 128)],
        [
            pltpu.VMEM((brick_z, wells), F32),
            pltpu.VMEM((1, wells), jnp.int32),
            pltpu.VMEM((1, wells), jnp.int32),
            pltpu.SemaphoreType.DMA((3,)),
        ],
        far=3,
    )
    received = lax.all_to_all(
        outgoing.reshape(owners, CAP, 128), ("gx", "gy"), split_axis=0, concat_axis=0, tiled=True
    ).reshape(CAP * owners, 128)

    flow = flow_sign.reshape(steps, rows, brick_y)
    speed = courant.reshape(3, rows, brick_y)
    trace = tracer.reshape(steps, rows, brick_y)
    field = (rows, brick_y)
    face_shapes = [(brick_z, brick_y)] * 2 + [(1, rows)] * 2 + [(brick_x, brick_y)]
    gradient = []
    adjoint, *faces = local(
        functools.partial(first_kernel, steps - 1),
        "first",
        [received, speed, flow],
        [field] + face_shapes,
        [
            pltpu.VMEM((3, *field), F32),
            pltpu.VMEM((1, *field), jnp.int32),
            pltpu.SemaphoreType.DMA((5,)),
        ],
        far=2,
    )
    for step in reversed(range(steps)):
        arrived = exchange(faces)
        if step == steps - 1:
            inputs, outputs, tracer_step = [], [], None
        else:
            inputs, outputs, tracer_step = [trace] + gradient, [field], step + 1
        *gradient, kept = local(
            functools.partial(inner_kernel, step, brick_z, tracer_step),
            f"inner{step}",
            [adjoint, speed, flow] + inputs,
            outputs + [field],
        )
        if step:
            adjoint, *faces = local(
                functools.partial(middle_kernel, sizes, step - 1),
                f"join{step}",
                [kept, *arrived, speed, flow],
                [field] + face_shapes,
            )
    adjoint, lines = local(
        functools.partial(last_kernel, sizes),
        "join0",
        [kept, *arrived, trace, *gradient],
        [field, field],
        [pltpu.VMEM(field, F32)],
    )
    y_lines = lax.all_to_all(
        lines.reshape(sizes[1], rows // sizes[1], brick_y), "gy", split_axis=0, concat_axis=0, tiled=True
    ).reshape(rows, brick_y)
    rows_each = sizes[1] * brick_y // devices
    (smooth,) = local(
        functools.partial(smooth_y_kernel, brick_z, 2.0 * brick_y, rows_each), "smooth_y", [y_lines], [field]
    )
    planes = lax.all_to_all(
        smooth.reshape(devices, 2, 128), axes, split_axis=0, concat_axis=0, tiled=True
    ).reshape(rows, brick_y)
    full_x, full_z = sizes[0] * brick_x, sizes[2] * brick_z
    (smoothed,) = local(
        functools.partial(smooth_xz_kernel, brick_z, 2.0 * brick_x, 2.0 * brick_z, rows_each),
        "smooth_xz",
        [planes],
        [(rows_each * full_z, full_x)],
        [pltpu.VMEM((rows_each * full_z, full_x), F32), pltpu.SemaphoreType.DMA((rows_each,))],
        far_out=True,
    )
    return (
        adjoint.reshape(brick_z, brick_x, brick_y),
        smoothed.reshape(rows_each, full_z, full_x),
    )


def solution(mesh):
    return jax.shard_map(
        per_device,
        mesh=mesh,
        in_specs=(
            P(("gx", "gy"), "gz"),
            P(("gx", "gy"), None),
            P(("gx", "gy")),
            P(None, "gz", "gx", "gy"),
            P(None, "gz", "gx", "gy"),
            P(None, "gz", "gx", "gy"),
        ),
        out_specs=(P("gz", "gx", "gy"), P(("gx", "gy", "gz"), None, None)),
        check_vma=False,
    )
```

```python
import functools
import math

import jax
import jax.numpy as jnp
from jax import lax
from jax.experimental import pallas as pl
from jax.experimental.pallas import tpu as pltpu
from jax.sharding import PartitionSpec as P

F32 = jnp.float32
BF16 = jnp.bfloat16
CAP = 2


def iota(shape, dim):
    return lax.broadcasted_iota(jnp.int32, shape, dim)


def thirds(value):
    high = value.astype(BF16)
    left = value - high.astype(F32)
    middle = left.astype(BF16)
    low = (left - middle.astype(F32)).astype(BF16)
    return high, middle, low


def halves(value):
    high = value.astype(BF16)
    return high, (value - high.astype(F32)).astype(BF16)


def dot(left, right, dims):
    return lax.dot_general(left, right, (dims, ((), ())), preferred_element_type=F32)


def dot3(left, right, dims):
    lh, ll = halves(left)
    rh, rl = halves(right)
    return dot(lh, rh, dims) + (dot(lh, rl, dims) + dot(ll, rh, dims))


def fetch(copies, sems):
    started = [pltpu.make_async_copy(source, target, sems.at[i]) for i, (source, target) in enumerate(copies)]
    for copy in started:
        copy.start()
    return started


def dispatch_kernel(sources_hbm, owner_hbm, cell_hbm, out_ref, sources_ref, owner_ref, cell_ref, sems):
    for copy in fetch([(sources_hbm, sources_ref), (owner_hbm, owner_ref), (cell_hbm, cell_ref)], sems):
        copy.wait()
    depth, wells = sources_ref.shape
    chunks, lanes = out_ref.shape
    owner = owner_ref[...]
    owner_row = owner.astype(F32)
    owner_col = jnp.transpose(jnp.broadcast_to(owner_row, (8, wells)))[:, :1]
    earlier = iota((wells, wells), 0) < iota((wells, wells), 1)
    same = (owner_col == owner_row) & earlier
    rank = jnp.sum(same.astype(F32), axis=0, keepdims=True)
    target = CAP * owner_row + rank
    chosen = jnp.where(iota((chunks, wells), 0).astype(F32) == target, 1.0, 0.0).astype(BF16)
    cell = jnp.broadcast_to(cell_ref[...].astype(F32), (lanes - depth, wells))
    total = jnp.zeros((chunks, lanes), F32)
    for piece in thirds(jnp.concatenate([sources_ref[...], cell], axis=0)):
        total = total + dot(chosen, piece, ((1,), (1,)))
    out_ref[...] = total


def landing(received_ref, depth, rows, lanes):
    wells, width = received_ref.shape
    across = rows // depth
    received = received_ref[...]
    cell = received[:, depth : depth + 1].astype(jnp.int32)
    spread = jnp.where(iota((width, rows), 0) == iota((width, rows), 1) // across, 1.0, 0.0).astype(BF16)
    at_x = iota((wells, rows), 1) % across == cell // lanes
    at_y = jnp.where(iota((wells, lanes), 1) == cell % lanes, 1.0, 0.0).astype(BF16)
    landed = jnp.zeros((rows, lanes), F32)
    for piece in reversed(thirds(received)):
        wide = jnp.where(at_x, dot(piece, spread, ((1,), (0,))), 0.0).astype(BF16)
        landed = landed + dot(wide, at_y, ((0,), (0,)))
    return landed


def put_faces(adjoint, step, courant_ref, sign_ref, depth, faces):
    rows, lanes = adjoint.shape
    across = rows // depth
    xe_ref, xo_ref, ye_ref, yo_ref, z_ref = faces
    sign = sign_ref[step]
    lane = iota((rows, lanes), 1)
    flow = courant_ref[1] * adjoint
    raised = (sign & 2) != 0
    ends = jnp.transpose(jnp.where(raised == (lane == 0), flow, 0.0))
    low, high = ends[0:1, :], ends[lanes - 1 : lanes, :]
    even = (lax.axis_index("gy") % 2) == 0
    ye_ref[...] = jnp.where(even, high, low)
    yo_ref[...] = jnp.where(even, low, high)
    shape = (depth, across, lanes)
    flow = (courant_ref[0] * adjoint).reshape(shape)
    raised = (sign & 1).reshape(shape)
    low = jnp.where(raised[:, 0, :] != 0, flow[:, 0, :], 0.0)
    high = jnp.where(raised[:, across - 1, :] != 0, 0.0, flow[:, across - 1, :])
    even = (lax.axis_index("gx") % 2) == 0
    xe_ref[...] = jnp.where(even, high, low)
    xo_ref[...] = jnp.where(even, low, high)
    flow = courant_ref[2]
    low = jnp.where((sign[:across] & 4) != 0, flow[:across] * adjoint[:across], 0.0)
    high = jnp.where((sign[rows - across :] & 4) != 0, 0.0, flow[rows - across :] * adjoint[rows - across :])
    z_ref[...] = jnp.where(lax.axis_index("gz") == 0, high, low)


def inner_kernel(step, depth, tracer_step, adjoint_ref, courant_ref, sign_ref, *rest):
    gradient_in, tracer_ref, gradient_ref = None, None, None
    if tracer_step is not None:
        tracer_ref, *rest = rest
        if len(rest) == 3:
            gradient_in, *rest = rest
        gradient_ref, *rest = rest
    (kept_ref,) = rest
    adjoint = adjoint_ref[...]
    rows, lanes = adjoint.shape
    across = rows // depth
    sign = sign_ref[step]
    row_x = iota((rows, lanes), 0) % across
    lane = iota((rows, lanes), 1)
    flow = [courant_ref[axis] * adjoint for axis in range(3)]
    rising = [jnp.where((sign & (1 << axis)) != 0, flow[axis], 0.0) for axis in range(3)]
    falling = [flow[axis] - rising[axis] for axis in range(3)]
    kept = (1.0 - (courant_ref[0] + courant_ref[1] + courant_ref[2])) * adjoint
    up = jnp.where(row_x == across - 1, 0.0, pltpu.roll(rising[0], rows - 1, 0))
    down = jnp.where(row_x == 0, 0.0, pltpu.roll(falling[0], 1, 0))
    kept = kept + up + down
    up = jnp.where(lane == lanes - 1, 0.0, pltpu.roll(rising[1], lanes - 1, 1))
    down = jnp.where(lane == 0, 0.0, pltpu.roll(falling[1], 1, 1))
    kept = kept + up + down
    blank = jnp.zeros((across, lanes), F32)
    kept_ref[...] = (
        kept
        + jnp.concatenate([rising[2][across:, :], blank], axis=0)
        + jnp.concatenate([blank, falling[2][: rows - across, :]], axis=0)
    )
    if tracer_step is not None:
        gradient = adjoint * tracer_ref[tracer_step]
        gradient_ref[...] = gradient if gradient_in is None else gradient_in[...] + gradient


def first_kernel(step, received_ref, courant_hbm, sign_hbm, *rest):
    adjoint_ref, *faces, courant_ref, sign_ref, sems = rest
    rows, lanes = adjoint_ref.shape
    depth = faces[0].shape[0]
    across = rows // depth
    last = rows - across
    copies = fetch(
        [
            (courant_hbm.at[1], courant_ref.at[1]),
            (sign_hbm.at[step], sign_ref.at[0]),
            (courant_hbm.at[0], courant_ref.at[0]),
            (courant_hbm.at[2, 0:across], courant_ref.at[2, 0:across]),
            (courant_hbm.at[2, last:rows], courant_ref.at[2, last:rows]),
        ],
        sems,
    )
    adjoint = landing(received_ref, depth, rows, lanes)
    adjoint_ref[...] = adjoint
    for copy in copies:
        copy.wait()
    put_faces(adjoint, 0, courant_ref, sign_ref, depth, faces)


def join(sizes, kept_ref, xe_ref, xo_ref, ye_ref, yo_ref, z_ref):
    rows, lanes = kept_ref.shape
    depth = xe_ref.shape[0]
    across = rows // depth
    gx, gy, gz = lax.axis_index("gx"), lax.axis_index("gy"), lax.axis_index("gz")
    even = (gx % 2) == 0
    xe, xo = xe_ref[...], xo_ref[...]
    above = jnp.where(gx == sizes[0] - 1, 0.0, jnp.where(even, xe, xo))
    below = jnp.where(gx == 0, 0.0, jnp.where(even, xo, xe))
    row_x = iota((depth, across, lanes), 1)
    adjoint = kept_ref[...] + jnp.where(
        row_x == across - 1,
        above[:, None, :],
        jnp.where(row_x == 0, below[:, None, :], 0.0),
    ).reshape(rows, lanes)
    even = (gy % 2) == 0
    ye, yo = ye_ref[...], yo_ref[...]
    above = jnp.where(gy == sizes[1] - 1, 0.0, jnp.where(even, ye, yo))
    below = jnp.where(gy == 0, 0.0, jnp.where(even, yo, ye))
    row_y = iota((lanes, rows), 0)
    adjoint = adjoint + jnp.transpose(
        jnp.where(row_y == lanes - 1, above, jnp.where(row_y == 0, below, 0.0))
    )
    z = z_ref[...]
    blank = jnp.zeros((rows - across, lanes), F32)
    return adjoint + jnp.where(
        gz == 0,
        jnp.concatenate([blank, z], axis=0),
        jnp.concatenate([z, blank], axis=0),
    )


def middle_kernel(sizes, step, kept_ref, xe, xo, ye, yo, z, courant_ref, sign_ref, adjoint_ref, *faces):
    adjoint = join(sizes, kept_ref, xe, xo, ye, yo, z)
    adjoint_ref[...] = adjoint
    put_faces(adjoint, step, courant_ref, sign_ref, xe.shape[0], faces)


def last_kernel(
    sizes, length, kept_ref, xe, xo, ye, yo, z, tracer_ref, gradient_in, adjoint_hbm, out_ref, work_ref, lines_ref, sem
):
    rows, lanes = kept_ref.shape
    depth = xe.shape[0]
    across = rows // depth
    adjoint = join(sizes, kept_ref, xe, xo, ye, yo, z)
    work_ref[...] = adjoint
    copy = pltpu.make_async_copy(work_ref, adjoint_hbm, sem)
    copy.start()
    lines_ref[...] = gradient_in[...] + adjoint * tracer_ref[0]
    lines = jnp.concatenate(
        [lines_ref[pl.ds(x, depth, stride=across), :] for x in range(across)], axis=0
    )
    rows_each = lanes // depth
    places = lanes // (sizes[1] * rows_each)
    group = sizes[1] * (places + 1)
    order = iota((rows_each * group, lanes), 0)
    r, j, e = order // group, order % group // (places + 1), order % (places + 1)
    y_out = y_of(sizes, lanes, rows_each, e, j, r)
    y_out = jnp.where(e < places, y_out, jnp.where(r == 0, lanes - 1, 0))
    table = jnp.exp(-jnp.abs(y_out - iota(order.shape, 1)).astype(F32) / length) * (1.0 / math.sqrt(length))
    result = dot3(table, lines, ((1,), (1,)))
    quarter = iota((group, lanes), 1) // depth
    for tile in range(rows // lanes):
        pieces = [result[r * group : (r + 1) * group, tile * lanes : (tile + 1) * lanes] for r in range(rows_each)]
        for u in range(rows_each):
            chunk = jnp.zeros((group, lanes), F32)
            for r in range(rows_each):
                turn = ((r - u) * depth) % lanes
                chunk = jnp.where(quarter == r, pltpu.roll(pieces[r], turn, 1) if turn else pieces[r], chunk)
            out_ref[pl.ds(tile * rows_each + u, group, stride=across), :] = chunk
    copy.wait()


def y_of(sizes, lanes, rows_each, place, gy, r):
    high, low = place // sizes[2], place % sizes[2]
    return high * (sizes[1] * sizes[2] * rows_each) + gy * (sizes[2] * rows_each) + low * rows_each + r


def carry_kernel(sizes, depth, across, length, lines_ref, out_ref):
    lanes = lines_ref.shape[1]
    bricks = sizes[1]
    rows_each = lanes // depth
    places = lanes // (bricks * rows_each)
    block = (places + 1) * across
    lane = iota((across, lanes), 1)

    def spread(values, group):
        values = jnp.where(lane // depth == group, values, 0.0)
        if group:
            values = pltpu.roll(values, lanes - group * depth, 1)
        step = depth
        while step < lanes:
            values = values + pltpu.roll(values, step, 1)
            step = 2 * step
        return values

    carries = [lines_ref[g * block + places * across : (g + 1) * block, :] for g in range(bricks)]
    decay = math.exp(-lanes / length)
    below, above = [None] * bricks, [None] * bricks
    total = jnp.zeros((across, lanes), F32)
    for g in range(bricks):
        below[g] = total
        total = decay * total + spread(carries[g], 0)
    total = jnp.zeros((across, lanes), F32)
    for g in reversed(range(bricks)):
        above[g] = total
        total = decay * total + spread(carries[g], 1)
    first_core = lax.axis_index("gz") == 0
    gy = lax.axis_index("gy")
    for high in range(places // sizes[2]):
        factors = []
        for low in range(sizes[2]):
            y = y_of(sizes, lanes, rows_each, high * sizes[2] + low, gy, iota((1, lanes), 1) // depth)
            y = y.astype(F32)
            factors.append((jnp.exp(-(y + 1.0) / length), jnp.exp(-(lanes - y) / length)))
        for g in range(bricks):
            values = []
            for low in range(sizes[2]):
                start = g * block + (high * sizes[2] + low) * across
                here = lines_ref[start : start + across, :]
                values.append(here + factors[low][0] * below[g] + factors[low][1] * above[g])
            start = (g * (places // sizes[2]) + high) * sizes[2] * across
            out_ref[start : start + across, :] = jnp.where(first_core, values[1], values[0])
            out_ref[start + across : start + 2 * across, :] = jnp.where(first_core, values[0], values[1])


def smooth_xz_kernel(depth, across, length_x, length_z, data_ref, other_ref, out_hbm, work_ref, sems):
    lanes = data_ref.shape[1]
    full_x = work_ref.shape[1]
    rows_each = lanes // depth
    gz = lax.axis_index("gz")
    x_in, x_out = iota((full_x, full_x), 0), iota((full_x, full_x), 1)
    table = jnp.exp(-jnp.abs(x_in - x_out).astype(F32) / length_x) * (1.0 / math.sqrt(length_x))
    own = jnp.concatenate(
        [data_ref[(2 * g + 1) * across : (2 * g + 2) * across, :] for g in range(full_x // across)], axis=0
    )
    own = dot3(own, table, ((0,), (0,)))
    other = dot3(other_ref[...], table, ((0,), (0,)))
    full_z = 2 * depth
    z_out, z_in = iota((full_z, full_z), 0), iota((full_z, full_z), 1)
    z_in = z_in % depth + jnp.where(z_in < depth, gz, 1 - gz) * depth
    table = jnp.exp(-jnp.abs(z_out - z_in).astype(F32) / length_z) * (1.0 / math.sqrt(length_z))
    copies = []
    for r in range(rows_each):
        part = slice(r * depth, (r + 1) * depth)
        column = jnp.concatenate([own[part], other[part]], axis=0)
        here = slice(r * full_z, (r + 1) * full_z)
        work_ref[here, :] = dot3(table, column, ((1,), (0,)))
        copy = pltpu.make_async_copy(work_ref.at[here], out_hbm.at[here], sems.at[r])
        copy.start()
        copies.append(copy)
    for copy in copies:
        copy.wait()


def pair_swaps(count):
    even = [(i, i ^ 1) for i in range(count)]
    odd = [(i, (i + 1) % count) for i in range(1, count, 2)]
    odd = odd + [(target, source) for source, target in odd]
    return even, odd


def exchange(faces):
    xe, xo, ye, yo, z = faces
    x_even, x_odd = pair_swaps(lax.axis_size("gx"))
    y_even, y_odd = pair_swaps(lax.axis_size("gy"))
    return (
        lax.ppermute(xe, "gx", x_even),
        lax.ppermute(xo, "gx", x_odd),
        lax.ppermute(ye, "gy", y_even),
        lax.ppermute(yo, "gy", y_odd),
        lax.ppermute(z, "gz", [(0, 1), (1, 0)]),
    )


def local(kernel, name, inputs, outputs, scratch=(), far=0, far_outputs=()):
    vmem = pl.BlockSpec(memory_space=pltpu.VMEM)
    hbm = pl.BlockSpec(memory_space=pl.ANY)
    near = len(inputs) - far
    out_far = [i in far_outputs for i in range(len(outputs))]
    return pl.pallas_call(
        kernel,
        in_specs=[vmem] * near + [hbm] * far,
        out_specs=[hbm if away else vmem for away in out_far],
        out_shape=[(pltpu.HBM if away else pltpu.VMEM)(dims, F32) for dims, away in zip(outputs, out_far)],
        scratch_shapes=scratch,
        compiler_params=pltpu.CompilerParams(vmem_limit_bytes=8 << 20),
        name=name,
    )(
        *[pltpu.with_memory_space_constraint(values, pltpu.VMEM) for values in inputs[:near]],
        *[pltpu.with_memory_space_constraint(values, pltpu.HBM) for values in inputs[near:]],
    )


def per_device(well_sources, well_owner, well_cell, flow_sign, courant, tracer):
    steps, brick_z, brick_x, brick_y = flow_sign.shape
    wells = well_sources.shape[0]
    rows = brick_z * brick_x
    sizes = (lax.axis_size("gx"), lax.axis_size("gy"), lax.axis_size("gz"))
    devices = sizes[0] * sizes[1] * sizes[2]
    owners = sizes[0] * sizes[1]
    axes = ("gx", "gy", "gz")
    (outgoing,) = local(
        dispatch_kernel,
        "dispatch",
        [well_sources.T, well_owner.reshape(1, wells), well_cell.reshape(1, wells)],
        [(CAP * owners, 128)],
        [
            pltpu.VMEM((brick_z, wells), F32),
            pltpu.VMEM((1, wells), jnp.int32),
            pltpu.VMEM((1, wells), jnp.int32),
            pltpu.SemaphoreType.DMA((3,)),
        ],
        far=3,
    )
    received = lax.all_to_all(
        outgoing.reshape(owners, CAP, 128), ("gx", "gy"), split_axis=0, concat_axis=0, tiled=True
    ).reshape(CAP * owners, 128)

    flow = flow_sign.reshape(steps, rows, brick_y)
    speed = courant.reshape(3, rows, brick_y)
    trace = tracer.reshape(steps, rows, brick_y)
    field = (rows, brick_y)
    face_shapes = [(brick_z, brick_y)] * 2 + [(1, rows)] * 2 + [(brick_x, brick_y)]
    gradient = []
    adjoint, *faces = local(
        functools.partial(first_kernel, steps - 1),
        "first",
        [received, speed, flow],
        [field] + face_shapes,
        [
            pltpu.VMEM((3, *field), F32),
            pltpu.VMEM((1, *field), jnp.int32),
            pltpu.SemaphoreType.DMA((5,)),
        ],
        far=2,
    )
    for step in reversed(range(steps)):
        arrived = exchange(faces)
        if step == steps - 1:
            inputs, outputs, tracer_step = [], [], None
        else:
            inputs, outputs, tracer_step = [trace] + gradient, [field], step + 1
        *gradient, kept = local(
            functools.partial(inner_kernel, step, brick_z, tracer_step),
            f"inner{step}",
            [adjoint, speed, flow] + inputs,
            outputs + [field],
        )
        if step:
            adjoint, *faces = local(
                functools.partial(middle_kernel, sizes, step - 1),
                f"join{step}",
                [kept, *arrived, speed, flow],
                [field] + face_shapes,
            )
    rows_each = sizes[1] * brick_y // devices
    block = (brick_y // (sizes[1] * rows_each) + 1) * brick_x
    length_y = 2.0 * brick_y
    adjoint, lines = local(
        functools.partial(last_kernel, sizes, length_y),
        "join0",
        [kept, *arrived, trace, *gradient],
        [field, (sizes[1] * block, brick_y)],
        [pltpu.VMEM(field, F32), pltpu.VMEM(field, F32), pltpu.SemaphoreType.DMA],
        far_outputs=(0,),
    )
    lines = lax.all_to_all(
        lines.reshape(sizes[1], block, brick_y), "gy", split_axis=0, concat_axis=0, tiled=True
    ).reshape(sizes[1] * block, brick_y)
    (planes,) = local(
        functools.partial(carry_kernel, sizes, brick_z, brick_x, length_y), "carry", [lines], [field]
    )
    planes = lax.all_to_all(
        planes.reshape(sizes[0], sizes[2] * brick_x, brick_y), "gx", split_axis=0, concat_axis=0, tiled=True
    )
    full_x, full_z = sizes[0] * brick_x, sizes[2] * brick_z
    other = lax.ppermute(planes[:, :brick_x], "gz", [(0, 1), (1, 0)])
    (smoothed,) = local(
        functools.partial(smooth_xz_kernel, brick_z, brick_x, 2.0 * brick_x, 2.0 * brick_z),
        "smooth_xz",
        [planes.reshape(field), other.reshape(full_x, brick_y)],
        [(rows_each * full_z, full_x)],
        [pltpu.VMEM((rows_each * full_z, full_x), F32), pltpu.SemaphoreType.DMA((rows_each,))],
        far_outputs=(0,),
    )
    return (
        adjoint.reshape(brick_z, brick_x, brick_y),
        smoothed.reshape(rows_each, full_z, full_x),
    )


def solution(mesh):
    return jax.shard_map(
        per_device,
        mesh=mesh,
        in_specs=(
            P(("gx", "gy"), "gz"),
            P(("gx", "gy"), None),
            P(("gx", "gy")),
            P(None, "gz", "gx", "gy"),
            P(None, "gz", "gx", "gy"),
            P(None, "gz", "gx", "gy"),
        ),
        out_specs=(P("gz", "gx", "gy"), P(("gx", "gy", "gz"), None, None)),
        check_vma=False,
    )
```

```python
import functools
import math

import jax
import jax.numpy as jnp
from jax import lax
from jax.experimental import pallas as pl
from jax.experimental.pallas import tpu as pltpu
from jax.sharding import PartitionSpec as P

F32 = jnp.float32
BF16 = jnp.bfloat16
CAP = 2


def iota(shape, dim):
    return lax.broadcasted_iota(jnp.int32, shape, dim)


def thirds(value):
    high = value.astype(BF16)
    left = value - high.astype(F32)
    middle = left.astype(BF16)
    low = (left - middle.astype(F32)).astype(BF16)
    return high, middle, low


def halves(value):
    high = value.astype(BF16)
    return high, (value - high.astype(F32)).astype(BF16)


def dot(left, right, dims):
    return lax.dot_general(left, right, (dims, ((), ())), preferred_element_type=F32)


def dot3(left, right, dims):
    lh, ll = halves(left)
    rh, rl = halves(right)
    return dot(lh, rh, dims) + (dot(lh, rl, dims) + dot(ll, rh, dims))


def fetch(copies, sems):
    started = [pltpu.make_async_copy(source, target, sems.at[i]) for i, (source, target) in enumerate(copies)]
    for copy in started:
        copy.start()
    return started


HALO = 3
PAD = 8
GROUP = 40


def open_kernel(sources_hbm, owner_hbm, cell_hbm, courant_hbm, sign_hbm, *rest):
    out_ref, even_ref, odd_ref, sources_ref, owner_ref, cell_ref, bits_ref, sems = rest
    gx, gy_count = lax.axis_index("gx"), lax.axis_size("gy")
    brick_x, brick_y = courant_hbm.shape[2], courant_hbm.shape[4]
    low, high = 0, brick_x - HALO
    is_even = (gx % 2) == 0
    first, second = jnp.where(is_even, high, low), jnp.where(is_even, low, high)
    copies = fetch(
        [
            (sources_hbm, sources_ref),
            (owner_hbm, owner_ref),
            (cell_hbm, cell_ref),
            (sign_hbm.at[:, :, pl.ds(first, HALO)], bits_ref.at[0]),
            (sign_hbm.at[:, :, pl.ds(second, HALO)], bits_ref.at[1]),
            (courant_hbm.at[:, :, pl.ds(first, HALO)], even_ref.at[0:3]),
            (courant_hbm.at[:, :, pl.ds(second, HALO)], odd_ref.at[0:3]),
        ],
        sems,
    )
    for copy in copies[:3]:
        copy.wait()
    depth, wells = sources_ref.shape
    chunks, lanes = out_ref.shape
    owner = owner_ref[...]
    owner_row = owner.astype(F32)
    owner_col = jnp.transpose(jnp.broadcast_to(owner_row, (8, wells)))[:, :1]
    earlier = iota((wells, wells), 0) < iota((wells, wells), 1)
    same = (owner_col == owner_row) & earlier
    rank = jnp.sum(same.astype(F32), axis=0, keepdims=True)
    cell = cell_ref[...]
    x = cell // brick_y
    far = float(-4 * chunks)
    target = CAP * owner_row + rank
    targets = [
        target,
        jnp.where(x >= high, target + CAP * gy_count, far),
        jnp.where(x < HALO, target - CAP * gy_count, far),
    ]
    row = iota((chunks, wells), 0).astype(F32)
    chosen = jnp.concatenate([jnp.where(row == t, 1.0, 0.0) for t in targets], axis=1).astype(BF16)
    column = jnp.concatenate(
        [sources_ref[...], jnp.broadcast_to(cell.astype(F32), (GROUP - depth, wells))], axis=0
    )
    payload = []
    for group in range(3):
        parts = [jnp.zeros((group * GROUP, wells), F32)] if group else []
        parts = parts + [column, jnp.zeros((lanes - (group + 1) * GROUP, wells), F32)]
        payload.append(jnp.concatenate(parts, axis=0))
    total = jnp.zeros((chunks, lanes), F32)
    for piece in thirds(jnp.concatenate(payload, axis=1)):
        total = total + dot(chosen, piece, ((1,), (1,)))
    out_ref[...] = total
    copies[3].wait()
    even_ref[3:6] = bits_ref[0].astype(F32)
    copies[4].wait()
    odd_ref[3:6] = bits_ref[1].astype(F32)
    copies[5].wait()
    copies[6].wait()


def load_kernel(gx_count, even_ref, odd_ref, courant_hbm, sign_hbm, courant_ref, sign_ref, sems):
    depth, across, lanes = courant_hbm.shape[1:]
    inside = slice(PAD, PAD + across)
    copies = fetch(
        [(courant_hbm.at[i], courant_ref.at[i, :, inside]) for i in range(3)]
        + [(sign_hbm.at[i], sign_ref.at[i, :, inside]) for i in range(3)],
        sems,
    )
    gx = lax.axis_index("gx")
    is_even = (gx % 2) == 0
    row = iota((depth, PAD, lanes), 1)
    for i in range(6):
        below = jnp.zeros((depth, PAD, lanes), F32)
        above = jnp.zeros((depth, PAD, lanes), F32)
        for d in range(HALO):
            xe = even_ref[i, pl.ds(d, depth, stride=HALO), :]
            xo = odd_ref[i, pl.ds(d, depth, stride=HALO), :]
            upper = jnp.where(gx == gx_count - 1, 0.0, jnp.where(is_even, xe, xo))
            lower = jnp.where(gx == 0, 0.0, jnp.where(is_even, xo, xe))
            above = jnp.where(row == d, upper[:, None, :], above)
            below = jnp.where(row == PAD - HALO + d, lower[:, None, :], below)
        if i < 3:
            courant_ref[i, :, 0:PAD] = below
            courant_ref[i, :, PAD + across :] = above
        else:
            sign_ref[i - 3, :, 0:PAD] = below.astype(jnp.int32)
            sign_ref[i - 3, :, PAD + across :] = above.astype(jnp.int32)
    for copy in copies:
        copy.wait()


def landing(received_ref, depth, across, lanes):
    wells, width = received_ref.shape
    pieces = thirds(received_ref[...])
    blocks = []
    for group, size, shift in ((1, PAD, across - PAD), (0, across, 0), (2, PAD, 0)):
        start, rows = group * GROUP, depth * size
        cell = received_ref[:, start + depth : start + depth + 1].astype(jnp.int32)
        spread = jnp.where(
            iota((width, rows), 0) == start + iota((width, rows), 1) // size, 1.0, 0.0
        ).astype(BF16)
        at_x = iota((wells, rows), 1) % size + shift == cell // lanes
        at_y = jnp.where(iota((wells, lanes), 1) == cell % lanes, 1.0, 0.0).astype(BF16)
        landed = jnp.zeros((rows, lanes), F32)
        for piece in reversed(pieces):
            wide = jnp.where(at_x, dot(piece, spread, ((1,), (0,))), 0.0).astype(BF16)
            landed = landed + dot(wide, at_y, ((0,), (0,)))
        blocks.append(landed.reshape(depth, size, lanes))
    return jnp.concatenate(blocks, axis=1).reshape(-1, lanes)


def flat(ref, index):
    return ref[index].reshape(-1, ref.shape[3])


def put_faces(adjoint, step, courant_ref, sign_ref, faces):
    rows, lanes = adjoint.shape
    wide = courant_ref.shape[2]
    ye_ref, yo_ref, z_ref = faces
    sign = flat(sign_ref, step)
    lane = iota((rows, lanes), 1)
    raised = (sign & 2) != 0
    ends = jnp.transpose(jnp.where(raised == (lane == 0), flat(courant_ref, 1) * adjoint, 0.0))
    low, high = ends[0:1, :], ends[lanes - 1 : lanes, :]
    even = (lax.axis_index("gy") % 2) == 0
    ye_ref[...] = jnp.where(even, high, low)
    yo_ref[...] = jnp.where(even, low, high)
    last = courant_ref.shape[1] - 1
    low = jnp.where((sign[:wide] & 4) != 0, courant_ref[2, 0] * adjoint[:wide], 0.0)
    high = jnp.where((sign[rows - wide :] & 4) != 0, 0.0, courant_ref[2, last] * adjoint[rows - wide :])
    z_ref[...] = jnp.where(lax.axis_index("gz") == 0, high, low)


def inside_of(values, wide):
    rows, lanes = values.shape
    values = values.reshape(rows // wide, wide, lanes)
    return values[:, PAD : wide - PAD].reshape(-1, lanes)


def inner_kernel(step, tracer_step, adjoint_ref, courant_ref, sign_ref, *rest):
    gradient_in, tracer_ref, gradient_ref = None, None, None
    if tracer_step is not None:
        tracer_ref, *rest = rest
        if len(rest) == 3:
            gradient_in, *rest = rest
        gradient_ref, *rest = rest
    (kept_ref,) = rest
    adjoint = adjoint_ref[...]
    rows, lanes = adjoint.shape
    wide = courant_ref.shape[2]
    sign = flat(sign_ref, step)
    speed = [flat(courant_ref, axis) for axis in range(3)]
    row_x = iota((rows, lanes), 0) % wide
    lane = iota((rows, lanes), 1)
    flow = [speed[axis] * adjoint for axis in range(3)]
    rising = [jnp.where((sign & (1 << axis)) != 0, flow[axis], 0.0) for axis in range(3)]
    falling = [flow[axis] - rising[axis] for axis in range(3)]
    kept = (1.0 - (speed[0] + speed[1] + speed[2])) * adjoint
    up = jnp.where(row_x == wide - 1, 0.0, pltpu.roll(rising[0], rows - 1, 0))
    down = jnp.where(row_x == 0, 0.0, pltpu.roll(falling[0], 1, 0))
    kept = kept + up + down
    up = jnp.where(lane == lanes - 1, 0.0, pltpu.roll(rising[1], lanes - 1, 1))
    down = jnp.where(lane == 0, 0.0, pltpu.roll(falling[1], 1, 1))
    kept = kept + up + down
    blank = jnp.zeros((wide, lanes), F32)
    kept_ref[...] = (
        kept
        + jnp.concatenate([rising[2][wide:, :], blank], axis=0)
        + jnp.concatenate([blank, falling[2][: rows - wide, :]], axis=0)
    )
    if tracer_step is not None:
        gradient = inside_of(adjoint, wide) * tracer_ref[tracer_step]
        gradient_ref[...] = gradient if gradient_in is None else gradient_in[...] + gradient


def first_kernel(step, received_ref, courant_ref, sign_ref, adjoint_ref, *faces):
    _, depth, wide, lanes = courant_ref.shape
    adjoint = landing(received_ref, depth, wide - 2 * PAD, lanes)
    adjoint_ref[...] = adjoint
    put_faces(adjoint, step, courant_ref, sign_ref, faces)


def join(sizes, kept_ref, ye_ref, yo_ref, z_ref):
    rows, lanes = kept_ref.shape
    wide = z_ref.shape[0]
    gy, gz = lax.axis_index("gy"), lax.axis_index("gz")
    even = (gy % 2) == 0
    ye, yo = ye_ref[...], yo_ref[...]
    above = jnp.where(gy == sizes[1] - 1, 0.0, jnp.where(even, ye, yo))
    below = jnp.where(gy == 0, 0.0, jnp.where(even, yo, ye))
    row_y = iota((lanes, rows), 0)
    adjoint = kept_ref[...] + jnp.transpose(
        jnp.where(row_y == lanes - 1, above, jnp.where(row_y == 0, below, 0.0))
    )
    z = z_ref[...]
    blank = jnp.zeros((rows - wide, lanes), F32)
    return adjoint + jnp.where(
        gz == 0,
        jnp.concatenate([blank, z], axis=0),
        jnp.concatenate([z, blank], axis=0),
    )


def middle_kernel(sizes, step, kept_ref, ye, yo, z, courant_ref, sign_ref, adjoint_ref, *faces):
    adjoint = join(sizes, kept_ref, ye, yo, z)
    adjoint_ref[...] = adjoint
    put_faces(adjoint, step, courant_ref, sign_ref, faces)


def last_kernel(
    sizes, length, depth, kept_ref, ye, yo, z, tracer_ref, gradient_in, adjoint_hbm, out_ref, work_ref, lines_ref, sem
):
    rows, lanes = work_ref.shape
    across = rows // depth
    adjoint = inside_of(join(sizes, kept_ref, ye, yo, z), z.shape[0])
    work_ref[...] = adjoint
    copy = pltpu.make_async_copy(work_ref, adjoint_hbm, sem)
    copy.start()
    lines_ref[...] = gradient_in[...] + adjoint * tracer_ref[0]
    lines = jnp.concatenate(
        [lines_ref[pl.ds(x, depth, stride=across), :] for x in range(across)], axis=0
    )
    rows_each = lanes // depth
    places = lanes // (sizes[1] * rows_each)
    group = sizes[1] * (places + 1)
    order = iota((rows_each * group, lanes), 0)
    r, j, e = order // group, order % group // (places + 1), order % (places + 1)
    y_out = y_of(sizes, lanes, rows_each, e, j, r)
    y_out = jnp.where(e < places, y_out, jnp.where(r == 0, lanes - 1, 0))
    table = jnp.exp(-jnp.abs(y_out - iota(order.shape, 1)).astype(F32) / length) * (1.0 / math.sqrt(length))
    result = dot3(table, lines, ((1,), (1,)))
    quarter = iota((group, lanes), 1) // depth
    for tile in range(rows // lanes):
        pieces = [result[r * group : (r + 1) * group, tile * lanes : (tile + 1) * lanes] for r in range(rows_each)]
        for u in range(rows_each):
            chunk = jnp.zeros((group, lanes), F32)
            for r in range(rows_each):
                turn = ((r - u) * depth) % lanes
                chunk = jnp.where(quarter == r, pltpu.roll(pieces[r], turn, 1) if turn else pieces[r], chunk)
            out_ref[pl.ds(tile * rows_each + u, group, stride=across), :] = chunk
    copy.wait()


def y_of(sizes, lanes, rows_each, place, gy, r):
    high, low = place // sizes[2], place % sizes[2]
    return high * (sizes[1] * sizes[2] * rows_each) + gy * (sizes[2] * rows_each) + low * rows_each + r


def carry_kernel(sizes, depth, across, length, lines_ref, out_ref):
    lanes = lines_ref.shape[1]
    bricks = sizes[1]
    rows_each = lanes // depth
    places = lanes // (bricks * rows_each)
    block = (places + 1) * across
    lane = iota((across, lanes), 1)

    def spread(values, group):
        values = jnp.where(lane // depth == group, values, 0.0)
        if group:
            values = pltpu.roll(values, lanes - group * depth, 1)
        step = depth
        while step < lanes:
            values = values + pltpu.roll(values, step, 1)
            step = 2 * step
        return values

    carries = [lines_ref[g * block + places * across : (g + 1) * block, :] for g in range(bricks)]
    decay = math.exp(-lanes / length)
    below, above = [None] * bricks, [None] * bricks
    total = jnp.zeros((across, lanes), F32)
    for g in range(bricks):
        below[g] = total
        total = decay * total + spread(carries[g], 0)
    total = jnp.zeros((across, lanes), F32)
    for g in reversed(range(bricks)):
        above[g] = total
        total = decay * total + spread(carries[g], 1)
    first_core = lax.axis_index("gz") == 0
    gy = lax.axis_index("gy")
    for high in range(places // sizes[2]):
        factors = []
        for low in range(sizes[2]):
            y = y_of(sizes, lanes, rows_each, high * sizes[2] + low, gy, iota((1, lanes), 1) // depth)
            y = y.astype(F32)
            factors.append((jnp.exp(-(y + 1.0) / length), jnp.exp(-(lanes - y) / length)))
        for g in range(bricks):
            values = []
            for low in range(sizes[2]):
                start = g * block + (high * sizes[2] + low) * across
                here = lines_ref[start : start + across, :]
                values.append(here + factors[low][0] * below[g] + factors[low][1] * above[g])
            start = (g * (places // sizes[2]) + high) * sizes[2] * across
            out_ref[start : start + across, :] = jnp.where(first_core, values[1], values[0])
            out_ref[start + across : start + 2 * across, :] = jnp.where(first_core, values[0], values[1])


def smooth_own_kernel(across, length, data_ref, own_ref, table_ref):
    full_x = own_ref.shape[1]
    x_in, x_out = iota((full_x, full_x), 0), iota((full_x, full_x), 1)
    table = jnp.exp(-jnp.abs(x_in - x_out).astype(F32) / length) * (1.0 / math.sqrt(length))
    table_ref[...] = table
    own = jnp.concatenate(
        [data_ref[(2 * g + 1) * across : (2 * g + 2) * across, :] for g in range(full_x // across)], axis=0
    )
    own_ref[...] = dot3(own, table, ((0,), (0,)))


def smooth_xz_kernel(depth, length, own_ref, table_ref, other_ref, out_hbm, work_ref, sems):
    rows_each = own_ref.shape[0] // depth
    gz = lax.axis_index("gz")
    own = own_ref[...]
    other = dot3(other_ref[...], table_ref[...], ((0,), (0,)))
    full_z = 2 * depth
    z_out, z_in = iota((full_z, full_z), 0), iota((full_z, full_z), 1)
    z_in = z_in % depth + jnp.where(z_in < depth, gz, 1 - gz) * depth
    table = jnp.exp(-jnp.abs(z_out - z_in).astype(F32) / length) * (1.0 / math.sqrt(length))
    copies = []
    for r in range(rows_each):
        part = slice(r * depth, (r + 1) * depth)
        column = jnp.concatenate([own[part], other[part]], axis=0)
        here = slice(r * full_z, (r + 1) * full_z)
        work_ref[here, :] = dot3(table, column, ((1,), (0,)))
        copy = pltpu.make_async_copy(work_ref.at[here], out_hbm.at[here], sems.at[r])
        copy.start()
        copies.append(copy)
    for copy in copies:
        copy.wait()


def pair_swaps(count):
    even = [(i, i ^ 1) for i in range(count)]
    odd = [(i, (i + 1) % count) for i in range(1, count, 2)]
    odd = odd + [(target, source) for source, target in odd]
    return even, odd


def swap(even, odd, axis):
    pairs = pair_swaps(lax.axis_size(axis))
    return lax.ppermute(even, axis, pairs[0]), lax.ppermute(odd, axis, pairs[1])


def exchange(faces):
    ye, yo, z = faces
    return (*swap(ye, yo, "gy"), lax.ppermute(z, "gz", [(0, 1), (1, 0)]))


def local(kernel, name, inputs, outputs, scratch=(), far=0, far_outputs=()):
    vmem = pl.BlockSpec(memory_space=pltpu.VMEM)
    hbm = pl.BlockSpec(memory_space=pl.ANY)
    near = len(inputs) - far
    out_far = [i in far_outputs for i in range(len(outputs))]
    return pl.pallas_call(
        kernel,
        in_specs=[vmem] * near + [hbm] * far,
        out_specs=[hbm if away else vmem for away in out_far],
        out_shape=[
            (pltpu.HBM if away else pltpu.VMEM)(*(dims if isinstance(dims[0], tuple) else (dims, F32)))
            for dims, away in zip(outputs, out_far)
        ],
        scratch_shapes=scratch,
        compiler_params=pltpu.CompilerParams(vmem_limit_bytes=12 << 20),
        name=name,
    )(
        *[pltpu.with_memory_space_constraint(values, pltpu.VMEM) for values in inputs[:near]],
        *[pltpu.with_memory_space_constraint(values, pltpu.HBM) for values in inputs[near:]],
    )


def per_device(well_sources, well_owner, well_cell, flow_sign, courant, tracer):
    steps, brick_z, brick_x, brick_y = flow_sign.shape
    wells = well_sources.shape[0]
    rows = brick_z * brick_x
    sizes = (lax.axis_size("gx"), lax.axis_size("gy"), lax.axis_size("gz"))
    devices = sizes[0] * sizes[1] * sizes[2]
    owners = sizes[0] * sizes[1]
    axes = ("gx", "gy", "gz")
    trace = tracer.reshape(steps, rows, brick_y)
    ends = (6, brick_z, HALO, 1, brick_y)
    lined = (3, brick_z, brick_x, 1, brick_y)
    outgoing, even, odd = local(
        open_kernel,
        "open",
        [
            well_sources.T,
            well_owner.reshape(1, wells),
            well_cell.reshape(1, wells),
            courant.reshape(lined),
            flow_sign.reshape(lined),
        ],
        [(CAP * owners, 128), ends, ends],
        [
            pltpu.VMEM((brick_z, wells), F32),
            pltpu.VMEM((1, wells), jnp.int32),
            pltpu.VMEM((1, wells), jnp.int32),
            pltpu.VMEM((2, 3, brick_z, HALO, 1, brick_y), jnp.int32),
            pltpu.SemaphoreType.DMA((7,)),
        ],
        far=5,
    )
    even, odd = swap(even, odd, "gx")
    received = lax.all_to_all(
        outgoing.reshape(owners, CAP, 128), ("gx", "gy"), split_axis=0, concat_axis=0, tiled=True
    ).reshape(CAP * owners, 128)
    wide_x = brick_x + 2 * PAD
    stack = (3, brick_z, wide_x, brick_y)
    weights = local(
        functools.partial(load_kernel, sizes[0]),
        "load",
        [
            even.reshape(6, brick_z * HALO, brick_y),
            odd.reshape(6, brick_z * HALO, brick_y),
            courant,
            flow_sign,
        ],
        [stack, (stack, jnp.int32)],
        [pltpu.SemaphoreType.DMA((6,))],
        far=2,
    )

    field = (rows, brick_y)
    wide = (brick_z * wide_x, brick_y)
    face_shapes = [(1, brick_z * wide_x)] * 2 + [(wide_x, brick_y)]
    gradient = []
    adjoint, *faces = local(
        functools.partial(first_kernel, steps - 1),
        "first",
        [received, *weights],
        [wide] + face_shapes,
    )
    for step in reversed(range(steps)):
        arrived = exchange(faces)
        if step == steps - 1:
            inputs, outputs, tracer_step = [], [], None
        else:
            inputs, outputs, tracer_step = [trace] + gradient, [field], step + 1
        *gradient, kept = local(
            functools.partial(inner_kernel, step, tracer_step),
            f"inner{step}",
            [adjoint, *weights] + inputs,
            outputs + [wide],
        )
        if step:
            adjoint, *faces = local(
                functools.partial(middle_kernel, sizes, step - 1),
                f"join{step}",
                [kept, *arrived, *weights],
                [wide] + face_shapes,
            )
    rows_each = sizes[1] * brick_y // devices
    block = (brick_y // (sizes[1] * rows_each) + 1) * brick_x
    length_y = 2.0 * brick_y
    adjoint, lines = local(
        functools.partial(last_kernel, sizes, length_y, brick_z),
        "join0",
        [kept, *arrived, trace, *gradient],
        [field, (sizes[1] * block, brick_y)],
        [pltpu.VMEM(field, F32), pltpu.VMEM(field, F32), pltpu.SemaphoreType.DMA],
        far_outputs=(0,),
    )
    lines = lax.all_to_all(
        lines.reshape(sizes[1], block, brick_y), "gy", split_axis=0, concat_axis=0, tiled=True
    ).reshape(sizes[1] * block, brick_y)
    (planes,) = local(
        functools.partial(carry_kernel, sizes, brick_z, brick_x, length_y), "carry", [lines], [field]
    )
    planes = lax.all_to_all(
        planes.reshape(sizes[0], sizes[2] * brick_x, brick_y), "gx", split_axis=0, concat_axis=0, tiled=True
    )
    full_x, full_z = sizes[0] * brick_x, sizes[2] * brick_z
    other = lax.ppermute(planes[:, :brick_x], "gz", [(0, 1), (1, 0)])
    own, table = local(
        functools.partial(smooth_own_kernel, brick_x, 2.0 * brick_x),
        "smooth_own",
        [planes.reshape(field)],
        [(brick_y, full_x), (full_x, full_x)],
    )
    (smoothed,) = local(
        functools.partial(smooth_xz_kernel, brick_z, 2.0 * brick_z),
        "smooth_xz",
        [own, table, other.reshape(full_x, brick_y)],
        [(rows_each * full_z, full_x)],
        [pltpu.VMEM((rows_each * full_z, full_x), F32), pltpu.SemaphoreType.DMA((rows_each,))],
        far_outputs=(0,),
    )
    return (
        adjoint.reshape(brick_z, brick_x, brick_y),
        smoothed.reshape(rows_each, full_z, full_x),
    )


def solution(mesh):
    return jax.shard_map(
        per_device,
        mesh=mesh,
        in_specs=(
            P(("gx", "gy"), "gz"),
            P(("gx", "gy"), None),
            P(("gx", "gy")),
            P(None, "gz", "gx", "gy"),
            P(None, "gz", "gx", "gy"),
            P(None, "gz", "gx", "gy"),
        ),
        out_specs=(P("gz", "gx", "gy"), P(("gx", "gy", "gz"), None, None)),
        check_vma=False,
    )
```

```python
import functools
import math

import jax
import jax.numpy as jnp
from jax import lax
from jax.experimental import pallas as pl
from jax.experimental.pallas import tpu as pltpu
from jax.sharding import PartitionSpec as P

F32 = jnp.float32
BF16 = jnp.bfloat16
CAP = 2


def iota(shape, dim):
    return lax.broadcasted_iota(jnp.int32, shape, dim)


def thirds(value):
    high = value.astype(BF16)
    left = value - high.astype(F32)
    middle = left.astype(BF16)
    low = (left - middle.astype(F32)).astype(BF16)
    return high, middle, low


def halves(value):
    high = value.astype(BF16)
    return high, (value - high.astype(F32)).astype(BF16)


def dot(left, right, dims):
    return lax.dot_general(left, right, (dims, ((), ())), preferred_element_type=F32)


def dot3(left, right, dims):
    lh, ll = halves(left)
    rh, rl = halves(right)
    return dot(lh, rh, dims) + (dot(lh, rl, dims) + dot(ll, rh, dims))


def fetch(copies, sems):
    started = [pltpu.make_async_copy(source, target, sems.at[i]) for i, (source, target) in enumerate(copies)]
    for copy in started:
        copy.start()
    return started


HALO = 3
PAD = 8
GROUP = 40


def open_kernel(sources_hbm, owner_hbm, cell_hbm, courant_hbm, sign_hbm, *rest):
    out_ref, even_ref, odd_ref, sources_ref, owner_ref, cell_ref, bits_ref, sems = rest
    gx, gy_count = lax.axis_index("gx"), lax.axis_size("gy")
    brick_x, brick_y = courant_hbm.shape[2], courant_hbm.shape[4]
    low, high = 0, brick_x - HALO
    is_even = (gx % 2) == 0
    first, second = jnp.where(is_even, high, low), jnp.where(is_even, low, high)
    copies = fetch(
        [
            (sources_hbm, sources_ref),
            (owner_hbm, owner_ref),
            (cell_hbm, cell_ref),
            (sign_hbm.at[:, :, pl.ds(first, HALO)], bits_ref.at[0]),
            (sign_hbm.at[:, :, pl.ds(second, HALO)], bits_ref.at[1]),
            (courant_hbm.at[:, :, pl.ds(first, HALO)], even_ref.at[0:3]),
            (courant_hbm.at[:, :, pl.ds(second, HALO)], odd_ref.at[0:3]),
        ],
        sems,
    )
    for copy in copies[:3]:
        copy.wait()
    depth, wells = sources_ref.shape
    chunks, lanes = out_ref.shape
    owner = owner_ref[...]
    owner_row = owner.astype(F32)
    owner_col = jnp.transpose(jnp.broadcast_to(owner_row, (8, wells)))[:, :1]
    earlier = iota((wells, wells), 0) < iota((wells, wells), 1)
    same = (owner_col == owner_row) & earlier
    rank = jnp.sum(same.astype(F32), axis=0, keepdims=True)
    cell = cell_ref[...]
    x = cell // brick_y
    far = float(-4 * chunks)
    spare = lanes - wells
    target = CAP * owner_row + rank
    targets = [
        target,
        jnp.where(x >= high, target + CAP * gy_count, far),
        jnp.where(x < HALO, target - CAP * gy_count, far),
    ]
    blank = jnp.full((1, spare), far, F32)
    row = iota((chunks, lanes), 0).astype(F32)
    chosen = jnp.concatenate(
        [jnp.where(row == jnp.concatenate([t, blank], axis=1), 1.0, 0.0).astype(BF16) for t in targets], axis=1
    )
    column = jnp.concatenate(
        [sources_ref[...], jnp.broadcast_to(cell.astype(F32), (GROUP - depth, wells))], axis=0
    )
    column = jnp.concatenate([column, jnp.zeros((GROUP, spare), F32)], axis=1)
    total = jnp.zeros((chunks, lanes), F32)
    for piece in thirds(column):
        payload = []
        for group in range(3):
            parts = [jnp.zeros((group * GROUP, lanes), F32)] if group else []
            parts = parts + [piece.astype(F32), jnp.zeros((lanes - (group + 1) * GROUP, lanes), F32)]
            payload.append(jnp.concatenate(parts, axis=0).astype(BF16))
        total = total + dot(chosen, jnp.concatenate(payload, axis=1), ((1,), (1,)))
    out_ref[...] = total
    copies[3].wait()
    even_ref[3:6] = bits_ref[0].astype(F32)
    copies[4].wait()
    odd_ref[3:6] = bits_ref[1].astype(F32)
    copies[5].wait()
    copies[6].wait()


def load_kernel(gx_count, even_ref, odd_ref, courant_hbm, sign_hbm, courant_ref, sign_ref, sems):
    depth, across, lanes = courant_hbm.shape[1:]
    inside = slice(PAD, PAD + across)
    copies = fetch(
        [(courant_hbm.at[i], courant_ref.at[i, :, inside]) for i in range(3)]
        + [(sign_hbm.at[i], sign_ref.at[i, :, inside]) for i in range(3)],
        sems,
    )
    gx = lax.axis_index("gx")
    is_even = (gx % 2) == 0
    row = iota((depth, PAD, lanes), 1)
    for i in range(6):
        below = jnp.zeros((depth, PAD, lanes), F32)
        above = jnp.zeros((depth, PAD, lanes), F32)
        for d in range(HALO):
            xe = even_ref[i, pl.ds(d, depth, stride=HALO), :]
            xo = odd_ref[i, pl.ds(d, depth, stride=HALO), :]
            upper = jnp.where(gx == gx_count - 1, 0.0, jnp.where(is_even, xe, xo))
            lower = jnp.where(gx == 0, 0.0, jnp.where(is_even, xo, xe))
            above = jnp.where(row == d, upper[:, None, :], above)
            below = jnp.where(row == PAD - HALO + d, lower[:, None, :], below)
        if i < 3:
            courant_ref[i, :, 0:PAD] = below
            courant_ref[i, :, PAD + across :] = above
        else:
            sign_ref[i - 3, :, 0:PAD] = below.astype(jnp.int32)
            sign_ref[i - 3, :, PAD + across :] = above.astype(jnp.int32)
    for copy in copies:
        copy.wait()


def landing(received_ref, depth, across, lanes):
    wells, width = received_ref.shape
    pieces = halves(received_ref[...])
    blocks = []
    for group, size, shift in ((1, PAD, across - PAD), (0, across, 0), (2, PAD, 0)):
        start, rows = group * GROUP, depth * size
        cell = received_ref[:, start + depth : start + depth + 1].astype(jnp.int32)
        spread = jnp.where(
            iota((width, rows), 0) == start + iota((width, rows), 1) // size, 1.0, 0.0
        ).astype(BF16)
        at_x = iota((wells, rows), 1) % size + shift == cell // lanes
        at_y = jnp.where(iota((wells, lanes), 1) == cell % lanes, 1.0, 0.0).astype(BF16)
        landed = jnp.zeros((rows, lanes), F32)
        for piece in reversed(pieces):
            wide = jnp.where(at_x, dot(piece, spread, ((1,), (0,))), 0.0).astype(BF16)
            landed = landed + dot(wide, at_y, ((0,), (0,)))
        blocks.append(landed.reshape(depth, size, lanes))
    return jnp.concatenate(blocks, axis=1).reshape(-1, lanes)


def flat(ref, index):
    return ref[index].reshape(-1, ref.shape[3])


def put_faces(adjoint, step, courant_ref, sign_ref, faces):
    rows, lanes = adjoint.shape
    wide = courant_ref.shape[2]
    ye_ref, yo_ref, z_ref = faces
    sign = flat(sign_ref, step)
    lane = iota((rows, lanes), 1)
    raised = (sign & 2) != 0
    ends = jnp.transpose(jnp.where(raised == (lane == 0), flat(courant_ref, 1) * adjoint, 0.0))
    low, high = ends[0:1, :], ends[lanes - 1 : lanes, :]
    even = (lax.axis_index("gy") % 2) == 0
    ye_ref[...] = jnp.where(even, high, low)
    yo_ref[...] = jnp.where(even, low, high)
    last = courant_ref.shape[1] - 1
    low = jnp.where((sign[:wide] & 4) != 0, courant_ref[2, 0] * adjoint[:wide], 0.0)
    high = jnp.where((sign[rows - wide :] & 4) != 0, 0.0, courant_ref[2, last] * adjoint[rows - wide :])
    z_ref[...] = jnp.where(lax.axis_index("gz") == 0, high, low)


def inside_of(values, wide):
    rows, lanes = values.shape
    values = values.reshape(rows // wide, wide, lanes)
    return values[:, PAD : wide - PAD].reshape(-1, lanes)


def inner_kernel(step, tracer_step, adjoint_ref, courant_ref, sign_ref, *rest):
    gradient_in, tracer_ref, gradient_ref = None, None, None
    if tracer_step is not None:
        tracer_ref, *rest = rest
        if len(rest) == 3:
            gradient_in, *rest = rest
        gradient_ref, *rest = rest
    (kept_ref,) = rest
    adjoint = adjoint_ref[...]
    rows, lanes = adjoint.shape
    wide = courant_ref.shape[2]
    sign = flat(sign_ref, step)
    speed = [flat(courant_ref, axis) for axis in range(3)]
    row_x = iota((rows, lanes), 0) % wide
    lane = iota((rows, lanes), 1)
    flow = [speed[axis] * adjoint for axis in range(3)]
    rising = [jnp.where((sign & (1 << axis)) != 0, flow[axis], 0.0) for axis in range(3)]
    falling = [flow[axis] - rising[axis] for axis in range(3)]
    kept = (1.0 - (speed[0] + speed[1] + speed[2])) * adjoint
    up = jnp.where(row_x == wide - 1, 0.0, pltpu.roll(rising[0], rows - 1, 0))
    down = jnp.where(row_x == 0, 0.0, pltpu.roll(falling[0], 1, 0))
    kept = kept + up + down
    up = jnp.where(lane == lanes - 1, 0.0, pltpu.roll(rising[1], lanes - 1, 1))
    down = jnp.where(lane == 0, 0.0, pltpu.roll(falling[1], 1, 1))
    kept = kept + up + down
    blank = jnp.zeros((wide, lanes), F32)
    kept_ref[...] = (
        kept
        + jnp.concatenate([rising[2][wide:, :], blank], axis=0)
        + jnp.concatenate([blank, falling[2][: rows - wide, :]], axis=0)
    )
    if tracer_step is not None:
        gradient = inside_of(adjoint, wide) * tracer_ref[tracer_step]
        gradient_ref[...] = gradient if gradient_in is None else gradient_in[...] + gradient


def first_kernel(step, received_ref, courant_ref, sign_ref, adjoint_ref, *faces):
    _, depth, wide, lanes = courant_ref.shape
    adjoint = landing(received_ref, depth, wide - 2 * PAD, lanes)
    adjoint_ref[...] = adjoint
    put_faces(adjoint, step, courant_ref, sign_ref, faces)


def join(sizes, kept_ref, ye_ref, yo_ref, z_ref):
    rows, lanes = kept_ref.shape
    wide = z_ref.shape[0]
    gy, gz = lax.axis_index("gy"), lax.axis_index("gz")
    even = (gy % 2) == 0
    ye, yo = ye_ref[...], yo_ref[...]
    above = jnp.where(gy == sizes[1] - 1, 0.0, jnp.where(even, ye, yo))
    below = jnp.where(gy == 0, 0.0, jnp.where(even, yo, ye))
    row_y = iota((lanes, rows), 0)
    adjoint = kept_ref[...] + jnp.transpose(
        jnp.where(row_y == lanes - 1, above, jnp.where(row_y == 0, below, 0.0))
    )
    z = z_ref[...]
    blank = jnp.zeros((rows - wide, lanes), F32)
    return adjoint + jnp.where(
        gz == 0,
        jnp.concatenate([blank, z], axis=0),
        jnp.concatenate([z, blank], axis=0),
    )


def middle_kernel(sizes, step, kept_ref, ye, yo, z, courant_ref, sign_ref, adjoint_ref, *faces):
    adjoint = join(sizes, kept_ref, ye, yo, z)
    adjoint_ref[...] = adjoint
    put_faces(adjoint, step, courant_ref, sign_ref, faces)


def last_kernel(
    sizes, length, depth, kept_ref, ye, yo, z, tracer_ref, gradient_in, adjoint_hbm, out_ref, work_ref, lines_ref, sem
):
    rows, lanes = work_ref.shape
    across = rows // depth
    adjoint = inside_of(join(sizes, kept_ref, ye, yo, z), z.shape[0])
    work_ref[...] = adjoint
    copy = pltpu.make_async_copy(work_ref, adjoint_hbm, sem)
    copy.start()
    lines_ref[...] = gradient_in[...] + adjoint * tracer_ref[0]
    lines = jnp.concatenate(
        [lines_ref[pl.ds(x, depth, stride=across), :] for x in range(across)], axis=0
    )
    rows_each = lanes // depth
    places = lanes // (sizes[1] * rows_each)
    group = sizes[1] * (places + 1)
    order = iota((rows_each * group, lanes), 0)
    r, j, e = order // group, order % group // (places + 1), order % (places + 1)
    y_out = y_of(sizes, lanes, rows_each, e, j, r)
    y_out = jnp.where(e < places, y_out, jnp.where(r == 0, lanes - 1, 0))
    table = jnp.exp(-jnp.abs(y_out - iota(order.shape, 1)).astype(F32) / length) * (1.0 / math.sqrt(length))
    result = dot3(table, lines, ((1,), (1,)))
    quarter = iota((group, lanes), 1) // depth
    for tile in range(rows // lanes):
        pieces = [result[r * group : (r + 1) * group, tile * lanes : (tile + 1) * lanes] for r in range(rows_each)]
        for u in range(rows_each):
            chunk = jnp.zeros((group, lanes), F32)
            for r in range(rows_each):
                turn = ((r - u) * depth) % lanes
                chunk = jnp.where(quarter == r, pltpu.roll(pieces[r], turn, 1) if turn else pieces[r], chunk)
            out_ref[pl.ds(tile * rows_each + u, group, stride=across), :] = chunk
    copy.wait()


def y_of(sizes, lanes, rows_each, place, gy, r):
    high, low = place // sizes[2], place % sizes[2]
    return high * (sizes[1] * sizes[2] * rows_each) + gy * (sizes[2] * rows_each) + low * rows_each + r


def carry_kernel(sizes, depth, across, length, lines_ref, out_ref):
    lanes = lines_ref.shape[1]
    bricks = sizes[1]
    rows_each = lanes // depth
    places = lanes // (bricks * rows_each)
    block = (places + 1) * across
    lane = iota((across, lanes), 1)

    def spread(values, group):
        values = jnp.where(lane // depth == group, values, 0.0)
        if group:
            values = pltpu.roll(values, lanes - group * depth, 1)
        step = depth
        while step < lanes:
            values = values + pltpu.roll(values, step, 1)
            step = 2 * step
        return values

    carries = [lines_ref[g * block + places * across : (g + 1) * block, :] for g in range(bricks)]
    decay = math.exp(-lanes / length)
    below, above = [None] * bricks, [None] * bricks
    total = jnp.zeros((across, lanes), F32)
    for g in range(bricks):
        below[g] = total
        total = decay * total + spread(carries[g], 0)
    total = jnp.zeros((across, lanes), F32)
    for g in reversed(range(bricks)):
        above[g] = total
        total = decay * total + spread(carries[g], 1)
    first_core = lax.axis_index("gz") == 0
    gy = lax.axis_index("gy")
    for high in range(places // sizes[2]):
        factors = []
        for low in range(sizes[2]):
            y = y_of(sizes, lanes, rows_each, high * sizes[2] + low, gy, iota((1, lanes), 1) // depth)
            y = y.astype(F32)
            factors.append((jnp.exp(-(y + 1.0) / length), jnp.exp(-(lanes - y) / length)))
        for g in range(bricks):
            values = []
            for low in range(sizes[2]):
                start = g * block + (high * sizes[2] + low) * across
                here = lines_ref[start : start + across, :]
                values.append(here + factors[low][0] * below[g] + factors[low][1] * above[g])
            start = (g * (places // sizes[2]) + high) * sizes[2] * across
            out_ref[start : start + across, :] = jnp.where(first_core, values[1], values[0])
            out_ref[start + across : start + 2 * across, :] = jnp.where(first_core, values[0], values[1])


def smooth_own_kernel(across, length, data_ref, own_ref, table_ref):
    full_x = own_ref.shape[1]
    x_in, x_out = iota((full_x, full_x), 0), iota((full_x, full_x), 1)
    table = jnp.exp(-jnp.abs(x_in - x_out).astype(F32) / length) * (1.0 / math.sqrt(length))
    table_ref[...] = table
    own = jnp.concatenate(
        [data_ref[(2 * g + 1) * across : (2 * g + 2) * across, :] for g in range(full_x // across)], axis=0
    )
    own_ref[...] = dot3(own, table, ((0,), (0,)))


def smooth_xz_kernel(depth, length, own_ref, table_ref, other_ref, out_hbm, work_ref, sems):
    rows_each = own_ref.shape[0] // depth
    gz = lax.axis_index("gz")
    own = own_ref[...]
    other = dot3(other_ref[...], table_ref[...], ((0,), (0,)))
    full_z = 2 * depth
    z_out, z_in = iota((full_z, full_z), 0), iota((full_z, full_z), 1)
    z_in = z_in % depth + jnp.where(z_in < depth, gz, 1 - gz) * depth
    table = jnp.exp(-jnp.abs(z_out - z_in).astype(F32) / length) * (1.0 / math.sqrt(length))
    copies = []
    for r in range(rows_each):
        part = slice(r * depth, (r + 1) * depth)
        column = jnp.concatenate([own[part], other[part]], axis=0)
        here = slice(r * full_z, (r + 1) * full_z)
        work_ref[here, :] = dot3(table, column, ((1,), (0,)))
        copy = pltpu.make_async_copy(work_ref.at[here], out_hbm.at[here], sems.at[r])
        copy.start()
        copies.append(copy)
    for copy in copies:
        copy.wait()


def pair_swaps(count):
    even = [(i, i ^ 1) for i in range(count)]
    odd = [(i, (i + 1) % count) for i in range(1, count, 2)]
    odd = odd + [(target, source) for source, target in odd]
    return even, odd


def swap(even, odd, axis):
    pairs = pair_swaps(lax.axis_size(axis))
    return lax.ppermute(even, axis, pairs[0]), lax.ppermute(odd, axis, pairs[1])


def exchange(faces):
    ye, yo, z = faces
    return (*swap(ye, yo, "gy"), lax.ppermute(z, "gz", [(0, 1), (1, 0)]))


def local(kernel, name, inputs, outputs, scratch=(), far=0, far_outputs=()):
    vmem = pl.BlockSpec(memory_space=pltpu.VMEM)
    hbm = pl.BlockSpec(memory_space=pl.ANY)
    near = len(inputs) - far
    out_far = [i in far_outputs for i in range(len(outputs))]
    return pl.pallas_call(
        kernel,
        in_specs=[vmem] * near + [hbm] * far,
        out_specs=[hbm if away else vmem for away in out_far],
        out_shape=[
            (pltpu.HBM if away else pltpu.VMEM)(*(dims if isinstance(dims[0], tuple) else (dims, F32)))
            for dims, away in zip(outputs, out_far)
        ],
        scratch_shapes=scratch,
        compiler_params=pltpu.CompilerParams(vmem_limit_bytes=12 << 20),
        name=name,
    )(
        *[pltpu.with_memory_space_constraint(values, pltpu.VMEM) for values in inputs[:near]],
        *[pltpu.with_memory_space_constraint(values, pltpu.HBM) for values in inputs[near:]],
    )


def per_device(well_sources, well_owner, well_cell, flow_sign, courant, tracer):
    steps, brick_z, brick_x, brick_y = flow_sign.shape
    wells = well_sources.shape[0]
    rows = brick_z * brick_x
    sizes = (lax.axis_size("gx"), lax.axis_size("gy"), lax.axis_size("gz"))
    devices = sizes[0] * sizes[1] * sizes[2]
    owners = sizes[0] * sizes[1]
    axes = ("gx", "gy", "gz")
    trace = tracer.reshape(steps, rows, brick_y)
    ends = (6, brick_z, HALO, 1, brick_y)
    lined = (3, brick_z, brick_x, 1, brick_y)
    outgoing, even, odd = local(
        open_kernel,
        "open",
        [
            well_sources.T,
            well_owner.reshape(1, wells),
            well_cell.reshape(1, wells),
            courant.reshape(lined),
            flow_sign.reshape(lined),
        ],
        [(CAP * owners, 128), ends, ends],
        [
            pltpu.VMEM((brick_z, wells), F32),
            pltpu.VMEM((1, wells), jnp.int32),
            pltpu.VMEM((1, wells), jnp.int32),
            pltpu.VMEM((2, 3, brick_z, HALO, 1, brick_y), jnp.int32),
            pltpu.SemaphoreType.DMA((7,)),
        ],
        far=5,
    )
    even, odd = swap(even, odd, "gx")
    received = lax.all_to_all(
        outgoing.reshape(owners, CAP, 128), ("gx", "gy"), split_axis=0, concat_axis=0, tiled=True
    ).reshape(CAP * owners, 128)
    wide_x = brick_x + 2 * PAD
    stack = (3, brick_z, wide_x, brick_y)
    weights = local(
        functools.partial(load_kernel, sizes[0]),
        "load",
        [
            even.reshape(6, brick_z * HALO, brick_y),
            odd.reshape(6, brick_z * HALO, brick_y),
            courant,
            flow_sign,
        ],
        [stack, (stack, jnp.int32)],
        [pltpu.SemaphoreType.DMA((6,))],
        far=2,
    )

    field = (rows, brick_y)
    wide = (brick_z * wide_x, brick_y)
    face_shapes = [(1, brick_z * wide_x)] * 2 + [(wide_x, brick_y)]
    gradient = []
    adjoint, *faces = local(
        functools.partial(first_kernel, steps - 1),
        "first",
        [received, *weights],
        [wide] + face_shapes,
    )
    for step in reversed(range(steps)):
        arrived = exchange(faces)
        if step == steps - 1:
            inputs, outputs, tracer_step = [], [], None
        else:
            inputs, outputs, tracer_step = [trace] + gradient, [field], step + 1
        *gradient, kept = local(
            functools.partial(inner_kernel, step, tracer_step),
            f"inner{step}",
            [adjoint, *weights] + inputs,
            outputs + [wide],
        )
        if step:
            adjoint, *faces = local(
                functools.partial(middle_kernel, sizes, step - 1),
                f"join{step}",
                [kept, *arrived, *weights],
                [wide] + face_shapes,
            )
    rows_each = sizes[1] * brick_y // devices
    block = (brick_y // (sizes[1] * rows_each) + 1) * brick_x
    length_y = 2.0 * brick_y
    adjoint, lines = local(
        functools.partial(last_kernel, sizes, length_y, brick_z),
        "join0",
        [kept, *arrived, trace, *gradient],
        [field, (sizes[1] * block, brick_y)],
        [pltpu.VMEM(field, F32), pltpu.VMEM(field, F32), pltpu.SemaphoreType.DMA],
        far_outputs=(0,),
    )
    lines = lax.all_to_all(
        lines.reshape(sizes[1], block, brick_y), "gy", split_axis=0, concat_axis=0, tiled=True
    ).reshape(sizes[1] * block, brick_y)
    (planes,) = local(
        functools.partial(carry_kernel, sizes, brick_z, brick_x, length_y), "carry", [lines], [field]
    )
    planes = lax.all_to_all(
        planes.reshape(sizes[0], sizes[2] * brick_x, brick_y), "gx", split_axis=0, concat_axis=0, tiled=True
    )
    full_x, full_z = sizes[0] * brick_x, sizes[2] * brick_z
    other = lax.ppermute(planes[:, :brick_x], "gz", [(0, 1), (1, 0)])
    own, table = local(
        functools.partial(smooth_own_kernel, brick_x, 2.0 * brick_x),
        "smooth_own",
        [planes.reshape(field)],
        [(brick_y, full_x), (full_x, full_x)],
    )
    (smoothed,) = local(
        functools.partial(smooth_xz_kernel, brick_z, 2.0 * brick_z),
        "smooth_xz",
        [own, table, other.reshape(full_x, brick_y)],
        [(rows_each * full_z, full_x)],
        [pltpu.VMEM((rows_each * full_z, full_x), F32), pltpu.SemaphoreType.DMA((rows_each,))],
        far_outputs=(0,),
    )
    return (
        adjoint.reshape(brick_z, brick_x, brick_y),
        smoothed.reshape(rows_each, full_z, full_x),
    )


def solution(mesh):
    return jax.shard_map(
        per_device,
        mesh=mesh,
        in_specs=(
            P(("gx", "gy"), "gz"),
            P(("gx", "gy"), None),
            P(("gx", "gy")),
            P(None, "gz", "gx", "gy"),
            P(None, "gz", "gx", "gy"),
            P(None, "gz", "gx", "gy"),
        ),
        out_specs=(P("gz", "gx", "gy"), P(("gx", "gy", "gz"), None, None)),
        check_vma=False,
    )
```

```python
import functools
import math

import jax
import jax.numpy as jnp
from jax import lax
from jax.experimental import pallas as pl
from jax.experimental.pallas import tpu as pltpu
from jax.sharding import PartitionSpec as P

F32 = jnp.float32
BF16 = jnp.bfloat16
CAP = 2


def iota(shape, dim):
    return lax.broadcasted_iota(jnp.int32, shape, dim)


def thirds(value):
    high = value.astype(BF16)
    left = value - high.astype(F32)
    middle = left.astype(BF16)
    low = (left - middle.astype(F32)).astype(BF16)
    return high, middle, low


def halves(value):
    high = value.astype(BF16)
    return high, (value - high.astype(F32)).astype(BF16)


def dot(left, right, dims):
    return lax.dot_general(left, right, (dims, ((), ())), preferred_element_type=F32)


def dot3(left, right, dims):
    lh, ll = halves(left)
    rh, rl = halves(right)
    return dot(lh, rh, dims) + (dot(lh, rl, dims) + dot(ll, rh, dims))


def fetch(copies, sems):
    started = [pltpu.make_async_copy(source, target, sems.at[i]) for i, (source, target) in enumerate(copies)]
    for copy in started:
        copy.start()
    return started


HALO = 3
PAD = 8
GROUP = 40


def open_kernel(sources_hbm, owner_hbm, cell_hbm, courant_hbm, sign_hbm, *rest):
    out_ref, even_ref, odd_ref, sources_ref, owner_ref, cell_ref, bits_ref, sems = rest
    gx, gy_count = lax.axis_index("gx"), lax.axis_size("gy")
    brick_x, brick_y = courant_hbm.shape[2], courant_hbm.shape[4]
    low, high = 0, brick_x - HALO
    is_even = (gx % 2) == 0
    first, second = jnp.where(is_even, high, low), jnp.where(is_even, low, high)
    copies = fetch(
        [
            (sources_hbm, sources_ref),
            (owner_hbm, owner_ref),
            (cell_hbm, cell_ref),
            (sign_hbm.at[:, :, pl.ds(first, HALO)], bits_ref.at[0]),
            (sign_hbm.at[:, :, pl.ds(second, HALO)], bits_ref.at[1]),
            (courant_hbm.at[:, :, pl.ds(first, HALO)], even_ref.at[0:3]),
            (courant_hbm.at[:, :, pl.ds(second, HALO)], odd_ref.at[0:3]),
        ],
        sems,
    )
    for copy in copies[:3]:
        copy.wait()
    depth, wells = sources_ref.shape
    chunks, lanes = out_ref.shape
    owner = owner_ref[...]
    owner_row = owner.astype(F32)
    owner_col = jnp.transpose(jnp.broadcast_to(owner_row, (8, wells)))[:, :1]
    earlier = iota((wells, wells), 0) < iota((wells, wells), 1)
    same = (owner_col == owner_row) & earlier
    rank = jnp.sum(same.astype(F32), axis=0, keepdims=True)
    cell = cell_ref[...]
    x = cell // brick_y
    far = float(-4 * chunks)
    spare = lanes - wells
    target = CAP * owner_row + rank
    targets = [
        target,
        jnp.where(x >= high, target + CAP * gy_count, far),
        jnp.where(x < HALO, target - CAP * gy_count, far),
    ]
    blank = jnp.full((1, spare), far, F32)
    row = iota((chunks, lanes), 0).astype(F32)
    chosen = jnp.concatenate(
        [jnp.where(row == jnp.concatenate([t, blank], axis=1), 1.0, 0.0).astype(BF16) for t in targets], axis=1
    )
    column = jnp.concatenate(
        [sources_ref[...], jnp.broadcast_to(cell.astype(F32), (GROUP - depth, wells))], axis=0
    )
    column = jnp.concatenate([column, jnp.zeros((GROUP, spare), F32)], axis=1)
    total = jnp.zeros((chunks, lanes), F32)
    for piece in thirds(column):
        payload = []
        for group in range(3):
            parts = [jnp.zeros((group * GROUP, lanes), F32)] if group else []
            parts = parts + [piece.astype(F32), jnp.zeros((lanes - (group + 1) * GROUP, lanes), F32)]
            payload.append(jnp.concatenate(parts, axis=0).astype(BF16))
        total = total + dot(chosen, jnp.concatenate(payload, axis=1), ((1,), (1,)))
    out_ref[...] = total
    copies[3].wait()
    even_ref[3:6] = bits_ref[0].astype(F32)
    copies[4].wait()
    odd_ref[3:6] = bits_ref[1].astype(F32)
    copies[5].wait()
    copies[6].wait()


def load_kernel(gx_count, even_ref, odd_ref, courant_hbm, sign_hbm, courant_ref, sign_ref, sems):
    depth, across, lanes = courant_hbm.shape[1:]
    inside = slice(PAD, PAD + across)
    copies = fetch(
        [(courant_hbm.at[i], courant_ref.at[i, :, inside]) for i in range(3)]
        + [(sign_hbm.at[i], sign_ref.at[i, :, inside]) for i in range(3)],
        sems,
    )
    gx = lax.axis_index("gx")
    is_even = (gx % 2) == 0
    row = iota((depth, PAD, lanes), 1)
    for i in range(6):
        below = jnp.zeros((depth, PAD, lanes), F32)
        above = jnp.zeros((depth, PAD, lanes), F32)
        for d in range(HALO):
            xe = even_ref[i, pl.ds(d, depth, stride=HALO), :]
            xo = odd_ref[i, pl.ds(d, depth, stride=HALO), :]
            upper = jnp.where(gx == gx_count - 1, 0.0, jnp.where(is_even, xe, xo))
            lower = jnp.where(gx == 0, 0.0, jnp.where(is_even, xo, xe))
            above = jnp.where(row == d, upper[:, None, :], above)
            below = jnp.where(row == PAD - HALO + d, lower[:, None, :], below)
        if i < 3:
            courant_ref[i, :, 0:PAD] = below
            courant_ref[i, :, PAD + across :] = above
        else:
            sign_ref[i - 3, :, 0:PAD] = below.astype(jnp.int32)
            sign_ref[i - 3, :, PAD + across :] = above.astype(jnp.int32)
    for copy in copies:
        copy.wait()


def landing(received_ref, depth, across, lanes):
    wells, width = received_ref.shape
    pieces = halves(received_ref[...])
    blocks = []
    for group, size, shift in ((1, PAD, across - PAD), (0, across, 0), (2, PAD, 0)):
        start, rows = group * GROUP, depth * size
        cell = received_ref[:, start + depth : start + depth + 1].astype(jnp.int32)
        spread = jnp.where(
            iota((width, rows), 0) == start + iota((width, rows), 1) // size, 1.0, 0.0
        ).astype(BF16)
        at_x = iota((wells, rows), 1) % size + shift == cell // lanes
        at_y = jnp.where(iota((wells, lanes), 1) == cell % lanes, 1.0, 0.0).astype(BF16)
        landed = jnp.zeros((rows, lanes), F32)
        for piece in reversed(pieces):
            wide = jnp.where(at_x, dot(piece, spread, ((1,), (0,))), 0.0).astype(BF16)
            landed = landed + dot(wide, at_y, ((0,), (0,)))
        blocks.append(landed.reshape(depth, size, lanes))
    return jnp.concatenate(blocks, axis=1).reshape(-1, lanes)


def flat(ref, index):
    return ref[index].reshape(-1, ref.shape[3])


def put_faces(adjoint, step, courant_ref, sign_ref, faces):
    rows, lanes = adjoint.shape
    wide = courant_ref.shape[2]
    ye_ref, yo_ref, z_ref = faces
    sign = flat(sign_ref, step)
    lane = iota((rows, lanes), 1)
    raised = (sign & 2) != 0
    ends = jnp.transpose(jnp.where(raised == (lane == 0), flat(courant_ref, 1) * adjoint, 0.0))
    low, high = ends[0:1, :], ends[lanes - 1 : lanes, :]
    even = (lax.axis_index("gy") % 2) == 0
    ye_ref[...] = jnp.where(even, high, low)
    yo_ref[...] = jnp.where(even, low, high)
    last = courant_ref.shape[1] - 1
    low = jnp.where((sign[:wide] & 4) != 0, courant_ref[2, 0] * adjoint[:wide], 0.0)
    high = jnp.where((sign[rows - wide :] & 4) != 0, 0.0, courant_ref[2, last] * adjoint[rows - wide :])
    z_ref[...] = jnp.where(lax.axis_index("gz") == 0, high, low)


def inside_of(values, wide):
    rows, lanes = values.shape
    values = values.reshape(rows // wide, wide, lanes)
    return values[:, PAD : wide - PAD].reshape(-1, lanes)


def inner_kernel(step, tracer_step, adjoint_ref, courant_ref, sign_ref, *rest):
    gradient_in, tracer_ref, gradient_ref = None, None, None
    if tracer_step is not None:
        tracer_ref, *rest = rest
        if len(rest) == 3:
            gradient_in, *rest = rest
        gradient_ref, *rest = rest
    (kept_ref,) = rest
    adjoint = adjoint_ref[...]
    rows, lanes = adjoint.shape
    wide = courant_ref.shape[2]
    sign = flat(sign_ref, step)
    speed = [flat(courant_ref, axis) for axis in range(3)]
    row_x = iota((rows, lanes), 0) % wide
    lane = iota((rows, lanes), 1)
    flow = [speed[axis] * adjoint for axis in range(3)]
    rising = [jnp.where((sign & (1 << axis)) != 0, flow[axis], 0.0) for axis in range(3)]
    falling = [flow[axis] - rising[axis] for axis in range(3)]
    kept = (1.0 - (speed[0] + speed[1] + speed[2])) * adjoint
    up = jnp.where(row_x == wide - 1, 0.0, pltpu.roll(rising[0], rows - 1, 0))
    down = jnp.where(row_x == 0, 0.0, pltpu.roll(falling[0], 1, 0))
    kept = kept + up + down
    up = jnp.where(lane == lanes - 1, 0.0, pltpu.roll(rising[1], lanes - 1, 1))
    down = jnp.where(lane == 0, 0.0, pltpu.roll(falling[1], 1, 1))
    kept = kept + up + down
    blank = jnp.zeros((wide, lanes), F32)
    kept_ref[...] = (
        kept
        + jnp.concatenate([rising[2][wide:, :], blank], axis=0)
        + jnp.concatenate([blank, falling[2][: rows - wide, :]], axis=0)
    )
    if tracer_step is not None:
        gradient = inside_of(adjoint, wide) * tracer_ref[tracer_step]
        gradient_ref[...] = gradient if gradient_in is None else gradient_in[...] + gradient


def first_kernel(step, received_ref, courant_ref, sign_ref, adjoint_ref, *faces):
    _, depth, wide, lanes = courant_ref.shape
    adjoint = landing(received_ref, depth, wide - 2 * PAD, lanes)
    adjoint_ref[...] = adjoint
    put_faces(adjoint, step, courant_ref, sign_ref, faces)


def join(sizes, kept_ref, ye_ref, yo_ref, z_ref):
    rows, lanes = kept_ref.shape
    wide = z_ref.shape[0]
    gy, gz = lax.axis_index("gy"), lax.axis_index("gz")
    even = (gy % 2) == 0
    ye, yo = ye_ref[...], yo_ref[...]
    above = jnp.where(gy == sizes[1] - 1, 0.0, jnp.where(even, ye, yo))
    below = jnp.where(gy == 0, 0.0, jnp.where(even, yo, ye))
    row_y = iota((lanes, rows), 0)
    adjoint = kept_ref[...] + jnp.transpose(
        jnp.where(row_y == lanes - 1, above, jnp.where(row_y == 0, below, 0.0))
    )
    z = z_ref[...]
    blank = jnp.zeros((rows - wide, lanes), F32)
    return adjoint + jnp.where(
        gz == 0,
        jnp.concatenate([blank, z], axis=0),
        jnp.concatenate([z, blank], axis=0),
    )


def middle_kernel(sizes, step, kept_ref, ye, yo, z, courant_ref, sign_ref, adjoint_ref, *faces):
    adjoint = join(sizes, kept_ref, ye, yo, z)
    adjoint_ref[...] = adjoint
    put_faces(adjoint, step, courant_ref, sign_ref, faces)


def last_kernel(
    sizes, length, depth, kept_ref, ye, yo, z, tracer_ref, gradient_in, adjoint_hbm, out_ref, work_ref, lines_ref, sem
):
    rows, lanes = work_ref.shape
    across = rows // depth
    adjoint = inside_of(join(sizes, kept_ref, ye, yo, z), z.shape[0])
    work_ref[...] = adjoint
    copy = pltpu.make_async_copy(work_ref, adjoint_hbm, sem)
    copy.start()
    lines_ref[...] = gradient_in[...] + adjoint * tracer_ref[0]
    lines = jnp.concatenate(
        [lines_ref[pl.ds(x, depth, stride=across), :] for x in range(across)], axis=0
    )
    rows_each = lanes // depth
    places = lanes // (sizes[1] * rows_each)
    group = sizes[1] * (places + 1)
    order = iota((rows_each * group, lanes), 0)
    r, j, e = order // group, order % group // (places + 1), order % (places + 1)
    y_out = y_of(sizes, rows_each, e, j, r)
    y_out = jnp.where(e < places, y_out, jnp.where(r == 0, lanes - 1, 0))
    table = jnp.exp(-jnp.abs(y_out - iota(order.shape, 1)).astype(F32) / length) * (1.0 / math.sqrt(length))
    result = dot3(table, lines, ((1,), (1,)))
    quarter = iota((group, lanes), 1) // depth
    for tile in range(rows // lanes):
        pieces = [result[r * group : (r + 1) * group, tile * lanes : (tile + 1) * lanes] for r in range(rows_each)]
        for u in range(rows_each):
            chunk = jnp.zeros((group, lanes), F32)
            for r in range(rows_each):
                turn = ((r - u) * depth) % lanes
                chunk = jnp.where(quarter == r, pltpu.roll(pieces[r], turn, 1) if turn else pieces[r], chunk)
            out_ref[pl.ds(tile * rows_each + u, group, stride=across), :] = chunk
    copy.wait()


def y_of(sizes, rows_each, place, gy, r):
    high, low = place // sizes[2], place % sizes[2]
    return high * (sizes[1] * sizes[2] * rows_each) + gy * (sizes[2] * rows_each) + low * rows_each + r


def carry_kernel(sizes, depth, across, length, lines_ref, out_ref):
    lanes = lines_ref.shape[1]
    bricks = sizes[1]
    rows_each = lanes // depth
    places = lanes // (bricks * rows_each)
    block = (places + 1) * across
    lane = iota((across, lanes), 1)

    def spread(values, group):
        values = jnp.where(lane // depth == group, values, 0.0)
        if group:
            values = pltpu.roll(values, lanes - group * depth, 1)
        step = depth
        while step < lanes:
            values = values + pltpu.roll(values, step, 1)
            step = 2 * step
        return values

    carries = [lines_ref[g * block + places * across : (g + 1) * block, :] for g in range(bricks)]
    decay = math.exp(-lanes / length)
    below, above = [None] * bricks, [None] * bricks
    total = jnp.zeros((across, lanes), F32)
    for g in range(bricks):
        below[g] = total
        total = decay * total + spread(carries[g], 0)
    total = jnp.zeros((across, lanes), F32)
    for g in reversed(range(bricks)):
        above[g] = total
        total = decay * total + spread(carries[g], 1)
    first_core = lax.axis_index("gz") == 0
    gy = lax.axis_index("gy")
    for high in range(places // sizes[2]):
        factors = []
        for low in range(sizes[2]):
            y = y_of(sizes, rows_each, high * sizes[2] + low, gy, iota((1, lanes), 1) // depth)
            y = y.astype(F32)
            factors.append((jnp.exp(-(y + 1.0) / length), jnp.exp(-(lanes - y) / length)))
        for g in range(bricks):
            values = []
            for low in range(sizes[2]):
                start = g * block + (high * sizes[2] + low) * across
                here = lines_ref[start : start + across, :]
                values.append(here + factors[low][0] * below[g] + factors[low][1] * above[g])
            start = (g * (places // sizes[2]) + high) * sizes[2] * across
            out_ref[start : start + across, :] = jnp.where(first_core, values[1], values[0])
            out_ref[start + across : start + 2 * across, :] = jnp.where(first_core, values[0], values[1])


def smooth_own_kernel(across, length, data_ref, own_ref, table_ref):
    full_x = own_ref.shape[1]
    x_in, x_out = iota((full_x, full_x), 0), iota((full_x, full_x), 1)
    table = jnp.exp(-jnp.abs(x_in - x_out).astype(F32) / length) * (1.0 / math.sqrt(length))
    table_ref[...] = table
    own = jnp.concatenate(
        [data_ref[(2 * g + 1) * across : (2 * g + 2) * across, :] for g in range(full_x // across)], axis=0
    )
    own_ref[...] = dot3(own, table, ((0,), (0,)))


def smooth_xz_kernel(depth, length, own_ref, table_ref, other_ref, out_hbm, work_ref, sems):
    rows_each = own_ref.shape[0] // depth
    gz = lax.axis_index("gz")
    own = own_ref[...]
    other = dot3(other_ref[...], table_ref[...], ((0,), (0,)))
    full_z = 2 * depth
    z_out, z_in = iota((full_z, full_z), 0), iota((full_z, full_z), 1)
    z_in = z_in % depth + jnp.where(z_in < depth, gz, 1 - gz) * depth
    table = jnp.exp(-jnp.abs(z_out - z_in).astype(F32) / length) * (1.0 / math.sqrt(length))
    copies = []
    for r in range(rows_each):
        part = slice(r * depth, (r + 1) * depth)
        column = jnp.concatenate([own[part], other[part]], axis=0)
        here = slice(r * full_z, (r + 1) * full_z)
        work_ref[here, :] = dot3(table, column, ((1,), (0,)))
        copy = pltpu.make_async_copy(work_ref.at[here], out_hbm.at[here], sems.at[r])
        copy.start()
        copies.append(copy)
    for copy in copies:
        copy.wait()


def pair_swaps(count):
    even = [(i, i ^ 1) for i in range(count)]
    odd = [(i, (i + 1) % count) for i in range(1, count, 2)]
    odd = odd + [(target, source) for source, target in odd]
    return even, odd


def swap(even, odd, axis):
    pairs = pair_swaps(lax.axis_size(axis))
    even = lax.ppermute(even, axis, pairs[0])
    odd = lax.ppermute(odd, axis, pairs[1])
    return even, odd


def exchange(faces):
    ye, yo, z = faces
    ye, yo = swap(ye, yo, "gy")
    z = lax.ppermute(z, "gz", [(0, 1), (1, 0)])
    return ye, yo, z


def local(kernel, inputs, outputs, scratch=(), far=0, far_outputs=()):
    vmem = pl.BlockSpec(memory_space=pltpu.VMEM)
    hbm = pl.BlockSpec(memory_space=pl.ANY)
    near = len(inputs) - far
    out_far = [i in far_outputs for i in range(len(outputs))]
    return pl.pallas_call(
        kernel,
        in_specs=[vmem] * near + [hbm] * far,
        out_specs=[hbm if away else vmem for away in out_far],
        out_shape=[
            (pltpu.HBM if away else pltpu.VMEM)(*(dims if isinstance(dims[0], tuple) else (dims, F32)))
            for dims, away in zip(outputs, out_far)
        ],
        scratch_shapes=scratch,
        compiler_params=pltpu.CompilerParams(vmem_limit_bytes=12 << 20),
    )(
        *[pltpu.with_memory_space_constraint(values, pltpu.VMEM) for values in inputs[:near]],
        *[pltpu.with_memory_space_constraint(values, pltpu.HBM) for values in inputs[near:]],
    )


def per_device(well_sources, well_owner, well_cell, flow_sign, courant, tracer):
    steps, brick_z, brick_x, brick_y = flow_sign.shape
    wells = well_sources.shape[0]
    rows = brick_z * brick_x
    sizes = (lax.axis_size("gx"), lax.axis_size("gy"), lax.axis_size("gz"))
    devices = sizes[0] * sizes[1] * sizes[2]
    owners = sizes[0] * sizes[1]
    trace = tracer.reshape(steps, rows, brick_y)
    ends = (6, brick_z, HALO, 1, brick_y)
    lined = (3, brick_z, brick_x, 1, brick_y)
    outgoing, even, odd = local(
        open_kernel,
        [
            well_sources.T,
            well_owner.reshape(1, wells),
            well_cell.reshape(1, wells),
            courant.reshape(lined),
            flow_sign.reshape(lined),
        ],
        [(CAP * owners, 128), ends, ends],
        [
            pltpu.VMEM((brick_z, wells), F32),
            pltpu.VMEM((1, wells), jnp.int32),
            pltpu.VMEM((1, wells), jnp.int32),
            pltpu.VMEM((2, 3, brick_z, HALO, 1, brick_y), jnp.int32),
            pltpu.SemaphoreType.DMA((7,)),
        ],
        far=5,
    )
    even, odd = swap(even, odd, "gx")
    received = lax.all_to_all(
        outgoing.reshape(owners, CAP, 128), ("gx", "gy"), split_axis=0, concat_axis=0, tiled=True
    ).reshape(CAP * owners, 128)
    wide_x = brick_x + 2 * PAD
    stack = (3, brick_z, wide_x, brick_y)
    weights = local(
        functools.partial(load_kernel, sizes[0]),
        [
            even.reshape(6, brick_z * HALO, brick_y),
            odd.reshape(6, brick_z * HALO, brick_y),
            courant,
            flow_sign,
        ],
        [stack, (stack, jnp.int32)],
        [pltpu.SemaphoreType.DMA((6,))],
        far=2,
    )

    field = (rows, brick_y)
    wide = (brick_z * wide_x, brick_y)
    face_shapes = [(1, brick_z * wide_x)] * 2 + [(wide_x, brick_y)]
    gradient = []
    adjoint, *faces = local(functools.partial(first_kernel, steps - 1), [received, *weights], [wide] + face_shapes)
    for step in reversed(range(steps)):
        arrived = exchange(faces)
        if step == steps - 1:
            inputs, outputs, tracer_step = [], [], None
        else:
            inputs, outputs, tracer_step = [trace] + gradient, [field], step + 1
        *gradient, kept = local(
            functools.partial(inner_kernel, step, tracer_step), [adjoint, *weights] + inputs, outputs + [wide]
        )
        if step:
            adjoint, *faces = local(
                functools.partial(middle_kernel, sizes, step - 1), [kept, *arrived, *weights], [wide] + face_shapes
            )
    rows_each = sizes[1] * brick_y // devices
    block = (brick_y // (sizes[1] * rows_each) + 1) * brick_x
    length_y = 2.0 * brick_y
    adjoint, lines = local(
        functools.partial(last_kernel, sizes, length_y, brick_z),
        [kept, *arrived, trace, *gradient],
        [field, (sizes[1] * block, brick_y)],
        [pltpu.VMEM(field, F32), pltpu.VMEM(field, F32), pltpu.SemaphoreType.DMA],
        far_outputs=(0,),
    )
    lines = lax.all_to_all(
        lines.reshape(sizes[1], block, brick_y), "gy", split_axis=0, concat_axis=0, tiled=True
    ).reshape(sizes[1] * block, brick_y)
    (planes,) = local(functools.partial(carry_kernel, sizes, brick_z, brick_x, length_y), [lines], [field])
    planes = lax.all_to_all(
        planes.reshape(sizes[0], sizes[2] * brick_x, brick_y), "gx", split_axis=0, concat_axis=0, tiled=True
    )
    full_x, full_z = sizes[0] * brick_x, sizes[2] * brick_z
    other = lax.ppermute(planes[:, :brick_x], "gz", [(0, 1), (1, 0)])
    own, table = local(
        functools.partial(smooth_own_kernel, brick_x, 2.0 * brick_x),
        [planes.reshape(field)],
        [(brick_y, full_x), (full_x, full_x)],
    )
    (smoothed,) = local(
        functools.partial(smooth_xz_kernel, brick_z, 2.0 * brick_z),
        [own, table, other.reshape(full_x, brick_y)],
        [(rows_each * full_z, full_x)],
        [pltpu.VMEM((rows_each * full_z, full_x), F32), pltpu.SemaphoreType.DMA((rows_each,))],
        far_outputs=(0,),
    )
    return (
        adjoint.reshape(brick_z, brick_x, brick_y),
        smoothed.reshape(rows_each, full_z, full_x),
    )


def solution(mesh):
    return jax.shard_map(
        per_device,
        mesh=mesh,
        in_specs=(
            P(("gx", "gy"), "gz"),
            P(("gx", "gy"), None),
            P(("gx", "gy")),
            P(None, "gz", "gx", "gy"),
            P(None, "gz", "gx", "gy"),
            P(None, "gz", "gx", "gy"),
        ),
        out_specs=(P("gz", "gx", "gy"), P(("gx", "gy", "gz"), None, None)),
        check_vma=False,
    )
```

```python
import functools
import math

import jax
import jax.numpy as jnp
from jax import lax
from jax.experimental import pallas as pl
from jax.experimental.pallas import tpu as pltpu
from jax.sharding import PartitionSpec as P

F32 = jnp.float32
BF16 = jnp.bfloat16
CAP = 2


def iota(shape, dim):
    return lax.broadcasted_iota(jnp.int32, shape, dim)


def thirds(value):
    high = value.astype(BF16)
    left = value - high.astype(F32)
    middle = left.astype(BF16)
    low = (left - middle.astype(F32)).astype(BF16)
    return high, middle, low


def halves(value):
    high = value.astype(BF16)
    return high, (value - high.astype(F32)).astype(BF16)


def dot(left, right, dims):
    return lax.dot_general(left, right, (dims, ((), ())), preferred_element_type=F32)


def dot3(left, right, dims):
    lh, ll = halves(left)
    rh, rl = halves(right)
    return dot(lh, rh, dims) + (dot(lh, rl, dims) + dot(ll, rh, dims))


def fetch(copies, sems):
    started = [pltpu.make_async_copy(source, target, sems.at[i]) for i, (source, target) in enumerate(copies)]
    for copy in started:
        copy.start()
    return started


HALO = 3
PAD = 8
GROUP = 40


def open_kernel(sources_hbm, owner_hbm, cell_hbm, courant_hbm, sign_hbm, *rest):
    out_ref, even_ref, odd_ref, sources_ref, owner_ref, cell_ref, bits_ref, sems = rest
    gx, gy_count = lax.axis_index("gx"), lax.axis_size("gy")
    brick_x, brick_y = courant_hbm.shape[2], courant_hbm.shape[4]
    low, high = 0, brick_x - HALO
    is_even = (gx % 2) == 0
    first, second = jnp.where(is_even, high, low), jnp.where(is_even, low, high)
    copies = fetch(
        [
            (sources_hbm, sources_ref),
            (owner_hbm, owner_ref),
            (cell_hbm, cell_ref),
            (sign_hbm.at[:, :, pl.ds(first, HALO)], bits_ref.at[0]),
            (sign_hbm.at[:, :, pl.ds(second, HALO)], bits_ref.at[1]),
            (courant_hbm.at[:, :, pl.ds(first, HALO)], even_ref.at[0:3]),
            (courant_hbm.at[:, :, pl.ds(second, HALO)], odd_ref.at[0:3]),
        ],
        sems,
    )
    for copy in copies[:3]:
        copy.wait()
    depth, wells = sources_ref.shape
    chunks, lanes = out_ref.shape
    owner = owner_ref[...]
    owner_row = owner.astype(F32)
    owner_col = jnp.transpose(jnp.broadcast_to(owner_row, (8, wells)))[:, :1]
    earlier = iota((wells, wells), 0) < iota((wells, wells), 1)
    same = (owner_col == owner_row) & earlier
    rank = jnp.sum(same.astype(F32), axis=0, keepdims=True)
    cell = cell_ref[...]
    x = cell // brick_y
    far = float(-4 * chunks)
    spare = lanes - wells
    target = CAP * owner_row + rank
    targets = [
        target,
        jnp.where(x >= high, target + CAP * gy_count, far),
        jnp.where(x < HALO, target - CAP * gy_count, far),
    ]
    blank = jnp.full((1, spare), far, F32)
    row = iota((chunks, lanes), 0).astype(F32)
    chosen = jnp.concatenate(
        [jnp.where(row == jnp.concatenate([t, blank], axis=1), 1.0, 0.0).astype(BF16) for t in targets], axis=1
    )
    column = jnp.concatenate(
        [sources_ref[...], jnp.broadcast_to(cell.astype(F32), (GROUP - depth, wells))], axis=0
    )
    column = jnp.concatenate([column, jnp.zeros((GROUP, spare), F32)], axis=1)
    total = jnp.zeros((chunks, lanes), F32)
    for piece in thirds(column):
        payload = []
        for group in range(3):
            parts = [jnp.zeros((group * GROUP, lanes), F32)] if group else []
            parts = parts + [piece.astype(F32), jnp.zeros((lanes - (group + 1) * GROUP, lanes), F32)]
            payload.append(jnp.concatenate(parts, axis=0).astype(BF16))
        total = total + dot(chosen, jnp.concatenate(payload, axis=1), ((1,), (1,)))
    out_ref[...] = total
    copies[3].wait()
    even_ref[3:6] = bits_ref[0].astype(F32)
    copies[4].wait()
    odd_ref[3:6] = bits_ref[1].astype(F32)
    copies[5].wait()
    copies[6].wait()


def load_kernel(gx_count, even_ref, odd_ref, courant_hbm, sign_hbm, courant_ref, sign_ref, sems):
    depth, across, lanes = courant_hbm.shape[1:]
    inside = slice(PAD, PAD + across)
    copies = fetch(
        [(courant_hbm.at[i], courant_ref.at[i, :, inside]) for i in range(3)]
        + [(sign_hbm.at[i], sign_ref.at[i, :, inside]) for i in range(3)],
        sems,
    )
    gx = lax.axis_index("gx")
    is_even = (gx % 2) == 0
    row = iota((depth, PAD, lanes), 1)
    for i in range(6):
        below = jnp.zeros((depth, PAD, lanes), F32)
        above = jnp.zeros((depth, PAD, lanes), F32)
        for d in range(HALO):
            xe = even_ref[i, pl.ds(d, depth, stride=HALO), :]
            xo = odd_ref[i, pl.ds(d, depth, stride=HALO), :]
            upper = jnp.where(gx == gx_count - 1, 0.0, jnp.where(is_even, xe, xo))
            lower = jnp.where(gx == 0, 0.0, jnp.where(is_even, xo, xe))
            above = jnp.where(row == d, upper[:, None, :], above)
            below = jnp.where(row == PAD - HALO + d, lower[:, None, :], below)
        if i < 3:
            courant_ref[i, :, 0:PAD] = below
            courant_ref[i, :, PAD + across :] = above
        else:
            sign_ref[i - 3, :, 0:PAD] = below.astype(jnp.int32)
            sign_ref[i - 3, :, PAD + across :] = above.astype(jnp.int32)
    for copy in copies:
        copy.wait()


def landing(received_ref, depth, across, lanes):
    wells, width = received_ref.shape
    pieces = halves(received_ref[...])
    blocks = []
    for group, size, shift in ((1, PAD, across - PAD), (0, across, 0), (2, PAD, 0)):
        start, rows = group * GROUP, depth * size
        cell = received_ref[:, start + depth : start + depth + 1].astype(jnp.int32)
        spread = jnp.where(
            iota((width, rows), 0) == start + iota((width, rows), 1) // size, 1.0, 0.0
        ).astype(BF16)
        at_x = iota((wells, rows), 1) % size + shift == cell // lanes
        at_y = jnp.where(iota((wells, lanes), 1) == cell % lanes, 1.0, 0.0).astype(BF16)
        landed = jnp.zeros((rows, lanes), F32)
        for piece in reversed(pieces):
            wide = jnp.where(at_x, dot(piece, spread, ((1,), (0,))), 0.0).astype(BF16)
            landed = landed + dot(wide, at_y, ((0,), (0,)))
        blocks.append(landed.reshape(depth, size, lanes))
    return jnp.concatenate(blocks, axis=1).reshape(-1, lanes)


def flat(ref, index):
    return ref[index].reshape(-1, ref.shape[3])


def put_faces(adjoint, step, courant_ref, sign_ref, faces):
    rows, lanes = adjoint.shape
    wide = courant_ref.shape[2]
    ye_ref, yo_ref, z_ref = faces
    sign = flat(sign_ref, step)
    lane = iota((rows, lanes), 1)
    raised = (sign & 2) != 0
    ends = jnp.transpose(jnp.where(raised == (lane == 0), flat(courant_ref, 1) * adjoint, 0.0))
    low, high = ends[0:1, :], ends[lanes - 1 : lanes, :]
    even = (lax.axis_index("gy") % 2) == 0
    ye_ref[...] = jnp.where(even, high, low)
    yo_ref[...] = jnp.where(even, low, high)
    last = courant_ref.shape[1] - 1
    low = jnp.where((sign[:wide] & 4) != 0, courant_ref[2, 0] * adjoint[:wide], 0.0)
    high = jnp.where((sign[rows - wide :] & 4) != 0, 0.0, courant_ref[2, last] * adjoint[rows - wide :])
    z_ref[...] = jnp.where(lax.axis_index("gz") == 0, high, low)


def inside_of(values, wide):
    rows, lanes = values.shape
    values = values.reshape(rows // wide, wide, lanes)
    return values[:, PAD : wide - PAD].reshape(-1, lanes)


def inner_kernel(step, tracer_step, adjoint_ref, courant_ref, sign_ref, *rest):
    gradient_in, tracer_ref, gradient_ref = None, None, None
    if tracer_step is not None:
        tracer_ref, *rest = rest
        if len(rest) == 3:
            gradient_in, *rest = rest
        gradient_ref, *rest = rest
    (kept_ref,) = rest
    adjoint = adjoint_ref[...]
    rows, lanes = adjoint.shape
    wide = courant_ref.shape[2]
    sign = flat(sign_ref, step)
    speed = [flat(courant_ref, axis) for axis in range(3)]
    row_x = iota((rows, lanes), 0) % wide
    lane = iota((rows, lanes), 1)
    flow = [speed[axis] * adjoint for axis in range(3)]
    rising = [jnp.where((sign & (1 << axis)) != 0, flow[axis], 0.0) for axis in range(3)]
    falling = [flow[axis] - rising[axis] for axis in range(3)]
    kept = (1.0 - (speed[0] + speed[1] + speed[2])) * adjoint
    up = jnp.where(row_x == wide - 1, 0.0, pltpu.roll(rising[0], rows - 1, 0))
    down = jnp.where(row_x == 0, 0.0, pltpu.roll(falling[0], 1, 0))
    kept = kept + up + down
    up = jnp.where(lane == lanes - 1, 0.0, pltpu.roll(rising[1], lanes - 1, 1))
    down = jnp.where(lane == 0, 0.0, pltpu.roll(falling[1], 1, 1))
    kept = kept + up + down
    blank = jnp.zeros((wide, lanes), F32)
    kept_ref[...] = (
        kept
        + jnp.concatenate([rising[2][wide:, :], blank], axis=0)
        + jnp.concatenate([blank, falling[2][: rows - wide, :]], axis=0)
    )
    if tracer_step is not None:
        gradient = inside_of(adjoint, wide) * tracer_ref[tracer_step]
        gradient_ref[...] = gradient if gradient_in is None else gradient_in[...] + gradient


def first_kernel(step, received_ref, courant_ref, sign_ref, adjoint_ref, *faces):
    _, depth, wide, lanes = courant_ref.shape
    adjoint = landing(received_ref, depth, wide - 2 * PAD, lanes)
    adjoint_ref[...] = adjoint
    put_faces(adjoint, step, courant_ref, sign_ref, faces)


def join(sizes, kept_ref, ye_ref, yo_ref, z_ref):
    rows, lanes = kept_ref.shape
    wide = z_ref.shape[0]
    gy, gz = lax.axis_index("gy"), lax.axis_index("gz")
    even = (gy % 2) == 0
    ye, yo = ye_ref[...], yo_ref[...]
    above = jnp.where(gy == sizes[1] - 1, 0.0, jnp.where(even, ye, yo))
    below = jnp.where(gy == 0, 0.0, jnp.where(even, yo, ye))
    row_y = iota((lanes, rows), 0)
    adjoint = kept_ref[...] + jnp.transpose(
        jnp.where(row_y == lanes - 1, above, jnp.where(row_y == 0, below, 0.0))
    )
    z = z_ref[...]
    blank = jnp.zeros((rows - wide, lanes), F32)
    return adjoint + jnp.where(
        gz == 0,
        jnp.concatenate([blank, z], axis=0),
        jnp.concatenate([z, blank], axis=0),
    )


def middle_kernel(sizes, step, kept_ref, ye, yo, z, courant_ref, sign_ref, adjoint_ref, *faces):
    adjoint = join(sizes, kept_ref, ye, yo, z)
    adjoint_ref[...] = adjoint
    put_faces(adjoint, step, courant_ref, sign_ref, faces)


def last_kernel(
    sizes, length, depth, kept_ref, ye, yo, z, tracer_ref, gradient_in, adjoint_hbm, out_ref, work_ref, lines_ref, sem
):
    rows, lanes = work_ref.shape
    across = rows // depth
    adjoint = inside_of(join(sizes, kept_ref, ye, yo, z), z.shape[0])
    work_ref[...] = adjoint
    copy = pltpu.make_async_copy(work_ref, adjoint_hbm, sem)
    copy.start()
    lines_ref[...] = gradient_in[...] + adjoint * tracer_ref[0]
    lines = jnp.concatenate(
        [lines_ref[pl.ds(x, depth, stride=across), :] for x in range(across)], axis=0
    )
    rows_each = lanes // depth
    places = lanes // (sizes[1] * rows_each)
    group = sizes[1] * (places + 1)
    order = iota((rows_each * group, lanes), 0)
    r, j, e = order // group, order % group // (places + 1), order % (places + 1)
    y_out = y_of(sizes, rows_each, e, j, r)
    y_out = jnp.where(e < places, y_out, jnp.where(r == 0, lanes - 1, 0))
    table = jnp.exp(-jnp.abs(y_out - iota(order.shape, 1)).astype(F32) / length) * (1.0 / math.sqrt(length))
    result = dot3(table, lines, ((1,), (1,)))
    quarter = iota((group, lanes), 1) // depth
    for tile in range(rows // lanes):
        pieces = [result[r * group : (r + 1) * group, tile * lanes : (tile + 1) * lanes] for r in range(rows_each)]
        for u in range(rows_each):
            chunk = jnp.zeros((group, lanes), F32)
            for r in range(rows_each):
                turn = ((r - u) * depth) % lanes
                chunk = jnp.where(quarter == r, pltpu.roll(pieces[r], turn, 1) if turn else pieces[r], chunk)
            out_ref[pl.ds(tile * rows_each + u, group, stride=across), :] = chunk
    copy.wait()


def y_of(sizes, rows_each, place, gy, r):
    high, low = place // sizes[2], place % sizes[2]
    return high * (sizes[1] * sizes[2] * rows_each) + gy * (sizes[2] * rows_each) + low * rows_each + r


def carry_kernel(sizes, depth, across, length, lines_ref, out_ref):
    lanes = lines_ref.shape[1]
    bricks = sizes[1]
    rows_each = lanes // depth
    places = lanes // (bricks * rows_each)
    block = (places + 1) * across
    lane = iota((across, lanes), 1)

    def spread(values, group):
        values = jnp.where(lane // depth == group, values, 0.0)
        if group:
            values = pltpu.roll(values, lanes - group * depth, 1)
        step = depth
        while step < lanes:
            values = values + pltpu.roll(values, step, 1)
            step = 2 * step
        return values

    carries = [lines_ref[g * block + places * across : (g + 1) * block, :] for g in range(bricks)]
    decay = math.exp(-lanes / length)
    below, above = [None] * bricks, [None] * bricks
    total = jnp.zeros((across, lanes), F32)
    for g in range(bricks):
        below[g] = total
        total = decay * total + spread(carries[g], 0)
    total = jnp.zeros((across, lanes), F32)
    for g in reversed(range(bricks)):
        above[g] = total
        total = decay * total + spread(carries[g], 1)
    first_core = lax.axis_index("gz") == 0
    gy = lax.axis_index("gy")
    for high in range(places // sizes[2]):
        factors = []
        for low in range(sizes[2]):
            y = y_of(sizes, rows_each, high * sizes[2] + low, gy, iota((1, lanes), 1) // depth)
            y = y.astype(F32)
            factors.append((jnp.exp(-(y + 1.0) / length), jnp.exp(-(lanes - y) / length)))
        for g in range(bricks):
            values = []
            for low in range(sizes[2]):
                start = g * block + (high * sizes[2] + low) * across
                here = lines_ref[start : start + across, :]
                values.append(here + factors[low][0] * below[g] + factors[low][1] * above[g])
            start = (g * (places // sizes[2]) + high) * sizes[2] * across
            out_ref[start : start + across, :] = jnp.where(first_core, values[1], values[0])
            out_ref[start + across : start + 2 * across, :] = jnp.where(first_core, values[0], values[1])


def depth_table(depth, length, core):
    z_out, z_in = iota((2 * depth, depth), 0), iota((2 * depth, depth), 1) + core * depth
    return jnp.exp(-jnp.abs(z_out - z_in).astype(F32) / length) * (1.0 / math.sqrt(length))


def smooth_own_kernel(depth, across, length_x, length_z, data_ref, sum_ref, high_ref, low_ref):
    full_x = sum_ref.shape[1]
    x_in, x_out = iota((full_x, full_x), 0), iota((full_x, full_x), 1)
    table = jnp.exp(-jnp.abs(x_in - x_out).astype(F32) / length_x) * (1.0 / math.sqrt(length_x))
    high_ref[...], low_ref[...] = halves(table)
    own = jnp.concatenate(
        [data_ref[(2 * g + 1) * across : (2 * g + 2) * across, :] for g in range(full_x // across)], axis=0
    )
    own = dot3(own, table, ((0,), (0,)))
    table = depth_table(depth, length_z, lax.axis_index("gz"))
    for r in range(own.shape[0] // depth):
        here = slice(2 * r * depth, 2 * (r + 1) * depth)
        sum_ref[here, :] = dot3(table, own[r * depth : (r + 1) * depth], ((1,), (0,)))


def smooth_xz_kernel(depth, length, sum_ref, high_ref, low_ref, other_ref, out_hbm, work_ref, sems):
    rows_each = other_ref.shape[1] // depth
    high, low = halves(other_ref[...])
    sides = ((0,), (0,))
    other = dot(high, high_ref[...], sides) + (dot(high, low_ref[...], sides) + dot(low, high_ref[...], sides))
    table = depth_table(depth, length, 1 - lax.axis_index("gz"))
    copies = []
    for r in range(rows_each):
        here = slice(2 * r * depth, 2 * (r + 1) * depth)
        work_ref[here, :] = sum_ref[here, :] + dot3(table, other[r * depth : (r + 1) * depth], ((1,), (0,)))
        copy = pltpu.make_async_copy(work_ref.at[here], out_hbm.at[here], sems.at[r])
        copy.start()
        copies.append(copy)
    for copy in copies:
        copy.wait()


def pair_swaps(count):
    even = [(i, i ^ 1) for i in range(count)]
    odd = [(i, (i + 1) % count) for i in range(1, count, 2)]
    odd = odd + [(target, source) for source, target in odd]
    return even, odd


def swap(even, odd, axis):
    pairs = pair_swaps(lax.axis_size(axis))
    even = lax.ppermute(even, axis, pairs[0])
    odd = lax.ppermute(odd, axis, pairs[1])
    return even, odd


def exchange(faces):
    ye, yo, z = faces
    ye, yo = swap(ye, yo, "gy")
    z = lax.ppermute(z, "gz", [(0, 1), (1, 0)])
    return ye, yo, z


def local(kernel, inputs, outputs, scratch=(), far=0, far_outputs=()):
    vmem = pl.BlockSpec(memory_space=pltpu.VMEM)
    hbm = pl.BlockSpec(memory_space=pl.ANY)
    near = len(inputs) - far
    out_far = [i in far_outputs for i in range(len(outputs))]
    return pl.pallas_call(
        kernel,
        in_specs=[vmem] * near + [hbm] * far,
        out_specs=[hbm if away else vmem for away in out_far],
        out_shape=[
            (pltpu.HBM if away else pltpu.VMEM)(*(dims if isinstance(dims[0], tuple) else (dims, F32)))
            for dims, away in zip(outputs, out_far)
        ],
        scratch_shapes=scratch,
        compiler_params=pltpu.CompilerParams(vmem_limit_bytes=12 << 20),
    )(
        *[pltpu.with_memory_space_constraint(values, pltpu.VMEM) for values in inputs[:near]],
        *[pltpu.with_memory_space_constraint(values, pltpu.HBM) for values in inputs[near:]],
    )


def per_device(well_sources, well_owner, well_cell, flow_sign, courant, tracer):
    steps, brick_z, brick_x, brick_y = flow_sign.shape
    wells = well_sources.shape[0]
    rows = brick_z * brick_x
    sizes = (lax.axis_size("gx"), lax.axis_size("gy"), lax.axis_size("gz"))
    devices = sizes[0] * sizes[1] * sizes[2]
    owners = sizes[0] * sizes[1]
    trace = tracer.reshape(steps, rows, brick_y)
    ends = (6, brick_z, HALO, 1, brick_y)
    lined = (3, brick_z, brick_x, 1, brick_y)
    outgoing, even, odd = local(
        open_kernel,
        [
            well_sources.T,
            well_owner.reshape(1, wells),
            well_cell.reshape(1, wells),
            courant.reshape(lined),
            flow_sign.reshape(lined),
        ],
        [(CAP * owners, 128), ends, ends],
        [
            pltpu.VMEM((brick_z, wells), F32),
            pltpu.VMEM((1, wells), jnp.int32),
            pltpu.VMEM((1, wells), jnp.int32),
            pltpu.VMEM((2, 3, brick_z, HALO, 1, brick_y), jnp.int32),
            pltpu.SemaphoreType.DMA((7,)),
        ],
        far=5,
    )
    even, odd = swap(even, odd, "gx")
    received = lax.all_to_all(
        outgoing.reshape(owners, CAP, 128), ("gx", "gy"), split_axis=0, concat_axis=0, tiled=True
    ).reshape(CAP * owners, 128)
    wide_x = brick_x + 2 * PAD
    stack = (3, brick_z, wide_x, brick_y)
    weights = local(
        functools.partial(load_kernel, sizes[0]),
        [
            even.reshape(6, brick_z * HALO, brick_y),
            odd.reshape(6, brick_z * HALO, brick_y),
            courant,
            flow_sign,
        ],
        [stack, (stack, jnp.int32)],
        [pltpu.SemaphoreType.DMA((6,))],
        far=2,
    )

    field = (rows, brick_y)
    wide = (brick_z * wide_x, brick_y)
    face_shapes = [(1, brick_z * wide_x)] * 2 + [(wide_x, brick_y)]
    gradient = []
    adjoint, *faces = local(functools.partial(first_kernel, steps - 1), [received, *weights], [wide] + face_shapes)
    for step in reversed(range(steps)):
        arrived = exchange(faces)
        if step == steps - 1:
            inputs, outputs, tracer_step = [], [], None
        else:
            inputs, outputs, tracer_step = [trace] + gradient, [field], step + 1
        *gradient, kept = local(
            functools.partial(inner_kernel, step, tracer_step), [adjoint, *weights] + inputs, outputs + [wide]
        )
        if step:
            adjoint, *faces = local(
                functools.partial(middle_kernel, sizes, step - 1), [kept, *arrived, *weights], [wide] + face_shapes
            )
    rows_each = sizes[1] * brick_y // devices
    block = (brick_y // (sizes[1] * rows_each) + 1) * brick_x
    length_y = 2.0 * brick_y
    adjoint, lines = local(
        functools.partial(last_kernel, sizes, length_y, brick_z),
        [kept, *arrived, trace, *gradient],
        [field, (sizes[1] * block, brick_y)],
        [pltpu.VMEM(field, F32), pltpu.VMEM(field, F32), pltpu.SemaphoreType.DMA],
        far_outputs=(0,),
    )
    lines = lax.all_to_all(
        lines.reshape(sizes[1], block, brick_y), "gy", split_axis=0, concat_axis=0, tiled=True
    ).reshape(sizes[1] * block, brick_y)
    (planes,) = local(functools.partial(carry_kernel, sizes, brick_z, brick_x, length_y), [lines], [field])
    planes = lax.all_to_all(
        planes.reshape(sizes[0], sizes[2] * brick_x, brick_y), "gx", split_axis=0, concat_axis=0, tiled=True
    )
    full_x, full_z = sizes[0] * brick_x, sizes[2] * brick_z
    other = lax.ppermute(planes[:, :brick_x], "gz", [(0, 1), (1, 0)])
    table = ((full_x, full_x), BF16)
    partial, high, low = local(
        functools.partial(smooth_own_kernel, brick_z, brick_x, 2.0 * brick_x, 2.0 * brick_z),
        [planes.reshape(field)],
        [(rows_each * full_z, full_x), table, table],
    )
    (smoothed,) = local(
        functools.partial(smooth_xz_kernel, brick_z, 2.0 * brick_z),
        [partial, high, low, other.reshape(full_x, brick_y)],
        [(rows_each * full_z, full_x)],
        [pltpu.VMEM((rows_each * full_z, full_x), F32), pltpu.SemaphoreType.DMA((rows_each,))],
        far_outputs=(0,),
    )
    return (
        adjoint.reshape(brick_z, brick_x, brick_y),
        smoothed.reshape(rows_each, full_z, full_x),
    )


def solution(mesh):
    return jax.shard_map(
        per_device,
        mesh=mesh,
        in_specs=(
            P(("gx", "gy"), "gz"),
            P(("gx", "gy"), None),
            P(("gx", "gy")),
            P(None, "gz", "gx", "gy"),
            P(None, "gz", "gx", "gy"),
            P(None, "gz", "gx", "gy"),
        ),
        out_specs=(P("gz", "gx", "gy"), P(("gx", "gy", "gz"), None, None)),
        check_vma=False,
    )
```
